32 devices in a mesh: groups: 2 (over x), outer: 4 (over z), inner: 4 (over y, core).
Axes of the slice: x: 2, y: 2, z: 4, core: 2. Of those that a mesh axis runs over, the one named last changes fastest.
Arguments:
- grid_feats: bfloat16 [16384, 1024], P(('groups', 'outer', 'inner')), parts along dimension 0, may hold values from -610 to 610
- mesh_feats: bfloat16 [8192, 1024], P(('groups', 'outer', 'inner')), parts along dimension 0, may hold values from -610 to 610
- routes: int32 [512, 4], P(('groups', 'outer', 'inner')), parts along dimension 0, may hold values from 0 to 15, all different within a row; in each aligned block of 16 rows (0 to 15, 16 to 31, ...) at most 4 rows name the same one
- edge_first: int32 [8192, 4], P(('groups', 'outer', 'inner')), parts along dimension 0, may hold values from 0 to 511, as said below
- edge_count: int32 [8192, 4], P(('groups', 'outer', 'inner')), parts along dimension 0, may hold values from 1 to 256
- w_query: bfloat16 [1024, 512], replicated, may hold values from -6 to 6
- w_kv: bfloat16 [1024, 1024], replicated, may hold values from -0.1875 to 0.1875
- w_out_enc: bfloat16 [512, 1024], replicated, may hold values from -2 to 2
- w_qkv: bfloat16 [1024, 1536], replicated, may hold values from -6 to 6
- w_out_proc: bfloat16 [512, 1024], replicated, may hold values from -2 to 2
Outputs:
- encoded: bfloat16 [8192, 1024], P(('groups', 'outer', 'inner')), parts along dimension 0
- processed: bfloat16 [8192, 1024], P(('groups', 'outer', 'inner')), parts along dimension 0
The draws below stay inside these ranges and needn't reach their ends.
There are 2 independent parts, one for each index of `groups`. The reference program is written for one: setup_inputs(seed, part) draws one part's arguments, and reference() takes and returns one part's arrays. A program takes and returns all parts, laid end to end along the dimension named above; an argument that names none is the same for every part. Nothing has to cross between parts.
Inputs may be any that keep to these rules, and one draw needn't show every extreme that they name: `routes`: in the rows of one device (16 blocks) no owner is named more than 4 times, a bound that some block reaches; each row names 4 different owners. edge_first + edge_count <= 512.
All inputs are finite; a program needn't handle non-finite values.
Results may differ from the reference program's by a relative error of at most 0.039.
Values may be sent and summed in bfloat16 or wider, within the bound.
No kernel may reach another device: no remote copies, remote signals or barrier semaphores. Data moves between devices by JAX's collectives and lax.ppermute only.
A program may use at most 64 MiB of HBM per device.

```python
import math
import jax
import jax.numpy as jnp
import numpy as np
from jax import lax

D = 1024
HEADS = 8
HD = 64
WIN = 512
TOP = 4
QB = 16
GRID_DEV = 512
QBLK = 16
CAP = 4
MESH_NODES = 4096
GRID_NODES = 8192
QBLOCKS = 256
KMAX = 256
N_OUTER = 4
N_INNER = 4


def span_pair(key):
    count_key = jax.random.fold_in(key, 11)
    first_key = jax.random.fold_in(key, 12)
    span_count = jax.random.randint(count_key, (MESH_NODES, TOP), 1, KMAX + 1)
    span_count = span_count.at[0, 0].set(KMAX).at[1, 0].set(1).at[2, 0].set(1)
    free_room = GRID_DEV - span_count + 1
    raw_bits = jax.random.randint(first_key, (MESH_NODES, TOP), 0, 1 << 20)
    span_first = raw_bits % free_room
    span_first = span_first.at[1, 0].set(GRID_DEV - 1).at[2, 0].set(0)
    return (span_first, span_count)


def draw_edge_first(key, part):
    return span_pair(key)[0]


def draw_edge_count(key, part):
    return span_pair(key)[1]


def feature_rows(key, row_count, tag):
    own_key = jax.random.fold_in(key, tag)
    values_raw = jnp.clip(jax.random.normal(jax.random.fold_in(own_key, 21), (row_count, D), jnp.float32), -6.0, 6.0)
    return values_raw.astype(jnp.bfloat16)


def draw_grid_feats(key, part):
    return feature_rows(key, GRID_NODES, 101)


def draw_mesh_feats(key, part):
    return feature_rows(key, MESH_NODES, 102)


def projection(key, columns, tag):
    own_key = jax.random.fold_in(key, tag)
    values_raw = jnp.clip(jax.random.normal(jax.random.fold_in(own_key, 31), (D, columns), jnp.float32), -4.0, 4.0) * D ** (-0.5)
    return jnp.clip(values_raw, -6.0, 6.0).astype(jnp.bfloat16)


def draw_w_query(key, part):
    return projection(key, HEADS * HD, 201)


def draw_w_qkv(key, part):
    return projection(key, 3 * HEADS * HD, 202)


def routed_block(rng, own, number, rows, count, top, reach, lean):
    ranking = jax.random.permutation(rng, count)
    crowded, common = shares(count, rows * top, reach, lean, True), shares(count, rows * top, reach, lean, False)
    places = jnp.arange(count)

    def named(tallies, turn):
        used = int((tallies > 0).sum())
        fixed = max(1, used // 4)
        moved = fixed + (places - fixed + turn * (used - fixed)) % max(1, count - fixed)
        return jnp.zeros((count,), jnp.int32).at[ranking[jnp.where(places < fixed, places, moved)]].set(jnp.asarray(tallies, jnp.int32))

    tallies = jnp.where(number % 4 == 0, named(crowded, number // 4), named(common, number - number // 4 - 1))
    mixed = jax.random.permutation(jax.random.fold_in(own, 3), count)
    source_of, receiver = mixed[0:count // 2 * 2:2], mixed[1:count // 2 * 2:2]
    slack = jnp.minimum(tallies[source_of] - 1, reach - tallies[receiver]) // 2
    slack = jnp.where((source_of == ranking[0]) | (receiver == ranking[0]) | (tallies[receiver] == 0), 0, jnp.maximum(slack, 0))
    moved = jax.random.randint(jax.random.fold_in(own, 4), (count // 2,), 0, 1 << 20) % (slack + 1)
    tallies = tallies.at[source_of].add(-moved).at[receiver].add(moved)
    items = jnp.searchsorted(jnp.cumsum(tallies), jnp.arange(rows * top), side="right").astype(jnp.int32)
    listing = items.reshape(top, rows).T
    listing = listing[jax.random.permutation(jax.random.fold_in(own, 1), rows)]
    turn = jax.random.randint(jax.random.fold_in(own, 2), (rows, 1), 0, top)
    return jnp.take_along_axis(listing, (jnp.arange(top)[None, :] + turn) % top, axis=1)


def shares(count, total, limit, slope, full):
    weights = [(1 << 20) // math.isqrt(grade ** slope) + 1 for grade in range(1, count + 1)]
    largest = limit if full else min(limit, max(-(-total // count), total * weights[0] // sum(weights)))
    least = 1 if total - largest >= count - 1 else 0
    holding, rest = [largest] + [least] * (count - 1), total - largest - least * (count - 1)
    while rest > 0:
        free = [i for i in range(1, count) if holding[i] < largest] or [i for i in range(1, count) if holding[i] < limit]
        whole, left = sum([weights[i] for i in free]), rest
        for i in free:
            addition = min(limit - holding[i], max(1, left * weights[i] // whole), rest)
            holding[i] = holding[i] + addition
            rest = rest - addition
    return np.array(holding)


def normal_values(stream_key, shape, width, reach, held_as=jnp.bfloat16):
    drawn = width * jax.random.normal(stream_key, shape, jnp.float32)
    return jnp.clip(drawn, min=-reach, max=reach).astype(held_as)


def setup_inputs(seed: int = 0, part: int = 0) -> dict:
    seeds = jax.random.split(jax.random.key(seed), 11)
    own_keys = jax.random.split(jax.random.fold_in(seeds[10], part), 11)
    grid_feats = draw_grid_feats(jax.random.fold_in(jax.random.fold_in(seeds[10], part), 71), part)
    mesh_feats = draw_mesh_feats(jax.random.fold_in(jax.random.fold_in(seeds[10], part), 71), part)
    routes_keys = jax.random.split(jax.random.fold_in(own_keys[2], 1), QBLOCKS // QBLK)
    routes_turns = jax.random.permutation(jax.random.fold_in(own_keys[2], 3), QBLOCKS // QBLK)
    routes = jax.vmap(lambda own, number: routed_block(jax.random.fold_in(own_keys[2], 2), own, number, QBLK, N_OUTER * N_INNER, TOP, CAP, 2))(routes_keys, routes_turns).reshape((QBLOCKS, TOP))
    edge_first = draw_edge_first(jax.random.fold_in(jax.random.fold_in(seeds[10], part), 71), part)
    edge_count = draw_edge_count(jax.random.fold_in(jax.random.fold_in(seeds[10], part), 71), part)
    w_query = draw_w_query(jax.random.fold_in(seeds[10], 71), part)
    w_kv = normal_values(seeds[6], (D, 2 * HEADS * HD), D ** -0.5, 0.1875)
    w_out_enc = normal_values(seeds[7], (HEADS * HD, D), HEADS ** -0.5, 2.0)
    w_qkv = draw_w_qkv(jax.random.fold_in(seeds[10], 71), part)
    w_out_proc = normal_values(seeds[9], (HEADS * HD, D), HEADS ** -0.5, 2.0)
    return dict(grid_feats=grid_feats, mesh_feats=mesh_feats, routes=routes, edge_first=edge_first, edge_count=edge_count, w_query=w_query, w_kv=w_kv, w_out_enc=w_out_enc, w_qkv=w_qkv, w_out_proc=w_out_proc)


def layer_norm(inputs):
    as_float = inputs.astype(jnp.float32)
    row_mean = lax.optimization_barrier(jnp.mean(as_float, axis=-1, keepdims=True))
    centered = as_float - row_mean
    variance = lax.optimization_barrier(jnp.mean(centered * centered, axis=-1, keepdims=True))
    return (centered * lax.rsqrt(variance + 1e-05)).astype(jnp.bfloat16)

def tile_partials(query_rows, span_first, span_count, key_rows, value_rows):
    row_count = query_rows.shape[0]
    head_dim = query_rows.shape[1] // HEADS
    key_count = key_rows.shape[0]
    query_heads = query_rows.astype(jnp.float32).reshape(row_count, HEADS, head_dim)
    key_heads = key_rows.astype(jnp.float32).reshape(key_count, HEADS, head_dim)
    value_heads = value_rows.astype(jnp.float32).reshape(key_count, HEADS, head_dim)
    scores = jnp.einsum('rhd,khd->rhk', query_heads, key_heads) * (1.0 / math.sqrt(head_dim))
    key_index = jnp.arange(key_count, dtype=jnp.int32)
    span_len = jnp.maximum(span_count, 1)
    allowed = (key_index[None, :] >= span_first[:, None]) & (key_index[None, :] < (span_first + span_len)[:, None])
    scores = jnp.where(allowed[:, None, :], scores, -jnp.inf)
    top_score = lax.optimization_barrier(jnp.max(scores, axis=-1))
    exp_terms = jnp.exp(scores - top_score[..., None])
    row_total = lax.optimization_barrier(jnp.sum(exp_terms, axis=-1))
    weights = exp_terms.astype(jnp.bfloat16)
    weighted = jnp.einsum('rhk,khd->rhd', weights.astype(jnp.float32), value_heads)
    partial_value = weighted / row_total[..., None]
    return (partial_value.reshape(row_count, HEADS * head_dim), top_score + jnp.log(row_total))

def window_block(query_block, key_block, key_base, node_total, half_window):
    row_count = query_block.shape[0]
    inner_width = query_block.shape[1]
    head_dim = inner_width // HEADS
    key_count = key_block.shape[0]
    query_heads = query_block.astype(jnp.float32).reshape(row_count, HEADS, head_dim)
    key_heads = key_block[:, :inner_width].astype(jnp.float32).reshape(key_count, HEADS, head_dim)
    value_heads = key_block[:, inner_width:].astype(jnp.float32).reshape(key_count, HEADS, head_dim)
    scores = jnp.einsum('qhd,khd->qhk', query_heads, key_heads) * (1.0 / math.sqrt(head_dim))
    query_pos = jnp.arange(row_count, dtype=jnp.int32)[:, None]
    key_pos = jnp.arange(key_count, dtype=jnp.int32)[None, :]
    key_global = key_base + key_pos
    allowed = (key_pos >= query_pos) & (key_pos < query_pos + 2 * half_window) & (key_global >= 0) & (key_global < node_total)
    scores = jnp.where(allowed[:, None, :], scores, -jnp.inf)
    top_score = lax.optimization_barrier(jnp.max(scores, axis=-1))
    exp_terms = jnp.exp(scores - top_score[..., None])
    probs = (exp_terms / lax.optimization_barrier(jnp.sum(exp_terms, axis=-1))[..., None]).astype(jnp.bfloat16)
    mixed_rows = jnp.einsum('qhk,khd->qhd', probs.astype(jnp.float32), value_heads)
    return mixed_rows.reshape(row_count, inner_width).astype(jnp.bfloat16)

def reference(grid_feats, mesh_feats, routes, edge_first, edge_count, w_query, w_kv, w_out_enc, w_qkv, w_out_proc):
    inner_width = HEADS * HD
    grid_kv = jnp.dot(layer_norm(grid_feats), w_kv, preferred_element_type=jnp.float32).astype(jnp.bfloat16)
    grid_keys = grid_kv[:, :inner_width]
    grid_values = grid_kv[:, inner_width:]
    queries = jnp.dot(layer_norm(mesh_feats), w_query, preferred_element_type=jnp.float32).astype(jnp.bfloat16)
    group = math.gcd(QBLOCKS, 16)
    query_blocks = queries.reshape(QBLOCKS // group, group, QB, inner_width)
    route_groups = routes.reshape(QBLOCKS // group, group, TOP)
    first_blocks = edge_first.reshape(QBLOCKS // group, group, QB, TOP)
    count_blocks = edge_count.reshape(QBLOCKS // group, group, QB, TOP)

    def encode(block_query, owners, first_cols, count_cols):

        def one_route(owner, first_col, count_col):
            row_start = (owner * GRID_DEV).astype(jnp.int32)
            key_rows = lax.dynamic_slice_in_dim(grid_keys, row_start, GRID_DEV, 0)
            value_rows = lax.dynamic_slice_in_dim(grid_values, row_start, GRID_DEV, 0)
            return tile_partials(block_query, first_col, count_col, key_rows, value_rows)
        partial_value, log_totals = jax.vmap(one_route, in_axes=(0, 1, 1))(owners, first_cols, count_cols)
        best_log = lax.optimization_barrier(jnp.max(log_totals, axis=0, keepdims=True))
        route_wts = jnp.exp(log_totals - best_log)
        partial_value = partial_value.reshape(TOP, QB, HEADS, HD)
        attended = lax.optimization_barrier(jnp.sum(route_wts[..., None] * partial_value, axis=0)) / lax.optimization_barrier(jnp.sum(route_wts, axis=0))[..., None]
        return attended.reshape(QB, inner_width).astype(jnp.bfloat16)

    def encode_group(inputs):
        return jax.vmap(encode)(inputs[0], inputs[1], inputs[2], inputs[3])
    attended = lax.map(encode_group, (query_blocks, route_groups, first_blocks, count_blocks)).reshape(MESH_NODES, inner_width)
    encoded = (mesh_feats.astype(jnp.float32) + jnp.dot(attended, w_out_enc, preferred_element_type=jnp.float32)).astype(jnp.bfloat16)
    proc_qkv = jnp.dot(layer_norm(encoded), w_qkv, preferred_element_type=jnp.float32).astype(jnp.bfloat16)
    proc_query = proc_qkv[:, :inner_width]
    window_kv = proc_qkv[:, inner_width:]
    half_window = WIN // 2
    padded = jnp.pad(window_kv, ((half_window, half_window), (0, 0)))
    block_rows = math.gcd(MESH_NODES, 512)

    def windowed(row_start):
        query_block = lax.dynamic_slice_in_dim(proc_query, row_start, block_rows, 0)
        key_block = lax.dynamic_slice_in_dim(padded, row_start, block_rows + 2 * half_window, 0)
        return window_block(query_block, key_block, row_start - half_window, MESH_NODES, half_window)
    starts = jnp.arange(MESH_NODES // block_rows, dtype=jnp.int32) * block_rows
    mixed_rows = lax.map(windowed, starts).reshape(MESH_NODES, inner_width)
    processed = (encoded.astype(jnp.float32) + jnp.dot(mixed_rows, w_out_proc, preferred_element_type=jnp.float32)).astype(jnp.bfloat16)
    return (encoded, processed)
```

```python
import functools
import math

import jax
import jax.numpy as jnp
from jax import lax
from jax.experimental import pallas as pl
from jax.experimental.pallas import tpu as pltpu
from jax.sharding import PartitionSpec as P

HEADS = 8
WIN = 512
LANES = 128
NEG = -1e30
AXES = ("outer", "inner")
VMEM = pl.BlockSpec(memory_space=pltpu.VMEM)
SMEM = pl.BlockSpec(memory_space=pltpu.SMEM)


def norm_rows(inputs):
    as_float = inputs.astype(jnp.float32)
    row_mean = jnp.mean(as_float, axis=-1, keepdims=True)
    centered = as_float - row_mean
    variance = jnp.mean(centered * centered, axis=-1, keepdims=True)
    return (centered * lax.rsqrt(variance + 1e-05)).astype(jnp.bfloat16)


def mm(a, b):
    return jnp.dot(a, b, preferred_element_type=jnp.float32)


def mm_nt(a, b):
    return lax.dot_general(a, b, (((1,), (1,)), ((), ())), preferred_element_type=jnp.float32)


def mm_tn(a, b):
    return lax.dot_general(a, b, (((0,), (0,)), ((), ())), preferred_element_type=jnp.float32)


def lane_group(shape, width):
    return lax.broadcasted_iota(jnp.int32, shape, len(shape) - 1) // width


def half_masks():
    low = (lane_group((1, LANES), LANES // 2) == 0).astype(jnp.float32)
    return low.astype(jnp.bfloat16), (1.0 - low).astype(jnp.bfloat16)


def send_kernel(block_len, capacity, head_scale, routes, first, count, mesh, w_query, send, ranks, tally, notes):
    route_count, block_count = routes.shape
    node_count = send.shape[0]
    pair_rows = capacity * block_len
    pairs = w_query.shape[1] // LANES
    note_rows = send.shape[1] - pairs * pair_rows
    queries = mm(norm_rows(mesh[...]), w_query[...]).astype(jnp.bfloat16)
    queries = queries * jnp.bfloat16(head_scale)
    if node_count * capacity != block_count * route_count:
        send[...] = jnp.zeros(send.shape, send.dtype)
    notes[...] = jnp.zeros(notes.shape, notes.dtype)
    first_all = first[...]
    upper = first_all >= 256
    low_part = jnp.where(upper, first_all - 256, first_all).astype(jnp.float32)
    signed = jnp.where(upper, -count[...], count[...]).astype(jnp.float32)
    group = lane_group((1, LANES), block_len)
    per_tile = LANES // block_len

    def clear(i, carry):
        tally[i] = 0
        return carry

    lax.fori_loop(0, node_count, clear, 0)
    for block in range(block_count):
        tile, spot = divmod(block, per_tile)
        cols = slice(tile * LANES, (tile + 1) * LANES)
        rows = slice(block * block_len, (block + 1) * block_len)
        for route in range(route_count):
            owner = routes[route, block]
            rank = tally[owner]
            tally[owner] = rank + 1
            ranks[route, block] = rank
            for pair in range(pairs):
                start = pl.multiple_of(pair * pair_rows + rank * block_len, block_len)
                send[owner, pl.ds(start, block_len), :] = queries[rows, pair * LANES:(pair + 1) * LANES]
            note = owner * note_rows + 2 * rank
            keep = group == spot
            notes[pl.ds(note, 1), :] = jnp.where(keep, low_part[route:route + 1, cols], 0.0)
            notes[pl.ds(note + 1, 1), :] = jnp.where(keep, signed[route:route + 1, cols], 0.0)
    for owner in range(node_count):
        send[owner, pairs * pair_rows:, :] = notes[owner * note_rows:(owner + 1) * note_rows, :].astype(jnp.bfloat16)


def grid_kernel(grid, w_kv, keys, values):
    width = w_kv.shape[1] // 2
    grid_kv = mm(norm_rows(grid[...]), w_kv[...]).astype(jnp.bfloat16)
    count = grid_kv.shape[0]
    masks = half_masks()
    for pair in range(width // LANES):
        key_pair = grid_kv[:, pair * LANES:(pair + 1) * LANES]
        value_pair = grid_kv[:, width + pair * LANES:width + (pair + 1) * LANES]
        for half in range(2):
            mask = masks[half]
            keys[2 * pair + half] = key_pair * mask
            values[pair, half * count:(half + 1) * count, :LANES] = value_pair * mask
            values[pair, half * count:(half + 1) * count, LANES:] = jnp.broadcast_to(mask, (count, LANES))


def owner_kernel(block_len, capacity, recv, keys, values, back, bias):
    node_count, message_rows, _ = recv.shape
    pairs, key_twice, _ = values.shape
    key_count = key_twice // 2
    pair_rows = capacity * block_len
    note_rows = message_rows - pairs * pair_rows
    row_count = node_count * pair_rows
    chunk = math.gcd(row_count, 256)
    group = chunk // pair_rows
    tags = recv[:, pairs * pair_rows:, :].reshape(node_count * note_rows, LANES)
    fold = (
        lax.broadcasted_iota(jnp.int32, (block_len, LANES), 1) % block_len
        == lax.broadcasted_iota(jnp.int32, (block_len, LANES), 0)
    ).astype(jnp.float32).astype(jnp.bfloat16)
    columns = mm_nt(fold, tags)
    key_pos = lax.broadcasted_iota(jnp.int32, (block_len, key_count), 1).astype(jnp.float32)
    for owner in range(node_count):
        for rank in range(capacity):
            spot = owner * note_rows + 2 * rank
            low_part, signed = columns[:, spot:spot + 1], columns[:, spot + 1:spot + 2]
            begin = low_part + jnp.where(signed < 0, 256.0, 0.0)
            end = begin + jnp.maximum(jnp.abs(signed), 1.0)
            inside = (key_pos >= begin) & (key_pos < end)
            row = (owner * capacity + rank) * block_len
            bias[row:row + block_len, :] = jnp.where(inside, 0.0, NEG)
    low_half = lane_group((chunk, LANES), LANES // 2) == 0
    pick_row = lax.broadcasted_iota(jnp.int32, (HEADS, LANES), 0)
    pick_lane = lax.broadcasted_iota(jnp.int32, (HEADS, LANES), 1)

    def step(index, carry):
        span = pl.ds(index * group, group)
        mask = bias[pl.ds(pl.multiple_of(index * chunk, chunk), chunk), :]
        log_high = jnp.zeros((HEADS, chunk), jnp.float32)
        log_low = jnp.zeros((HEADS, chunk), jnp.float32)
        for pair in range(pairs):
            part = slice(pair * pair_rows, (pair + 1) * pair_rows)
            query_pair = recv[span, part, :].reshape(chunk, LANES)
            tops, terms = [], []
            for half in range(2):
                scores = mm_nt(query_pair, keys[2 * pair + half]) + mask
                top = jnp.max(scores, axis=-1, keepdims=True)
                tops.append(top)
                terms.append(jnp.exp(scores - top).astype(jnp.bfloat16))
            mixed = mm(jnp.concatenate(terms, axis=1), values[pair])
            total = mixed[:, LANES:]
            back[span, part, :] = (mixed[:, :LANES] / total).astype(jnp.bfloat16).reshape(group, pair_rows, LANES)
            logs = jnp.where(low_half, tops[0], tops[1]) + jnp.log(total)
            high = logs.astype(jnp.bfloat16)
            low = (logs - high.astype(jnp.float32)).astype(jnp.bfloat16)
            pick = (
                ((pick_row == 2 * pair) & (pick_lane == 0)) | ((pick_row == 2 * pair + 1) & (pick_lane == LANES // 2))
            ).astype(jnp.float32).astype(jnp.bfloat16)
            log_high = log_high + mm_nt(pick, high)
            log_low = log_low + mm_nt(pick, low)
        half_lane = lane_group((HEADS, LANES), LANES // 2)
        for offset in range(group):
            lane = offset * pair_rows
            tile, shift = lane // LANES, lane % LANES
            high = log_high[:, tile * LANES:(tile + 1) * LANES]
            low = log_low[:, tile * LANES:(tile + 1) * LANES]
            if shift:
                high = pltpu.roll(high, LANES - shift, 1)
            low_shift = (LANES // 2 - shift) % LANES
            if low_shift:
                low = pltpu.roll(low, low_shift, 1)
            back[index * group + offset, pairs * pair_rows:pairs * pair_rows + HEADS, :] = jnp.where(
                half_lane == 0, high, low
            ).astype(jnp.bfloat16)
        return carry

    lax.fori_loop(0, row_count // chunk, step, 0)


def combine_kernel(block_len, capacity, routes, ranks, back, attended, logs):
    route_count, block_count = routes.shape
    node_count, message_rows, _ = back.shape
    width = attended.shape[1]
    pairs = width // LANES
    pair_rows = capacity * block_len
    halves = back[:, pairs * pair_rows:pairs * pair_rows + HEADS, :].astype(jnp.float32).reshape(node_count * HEADS, LANES)
    logs[...] = halves + pltpu.roll(halves, LANES // 2, 1)
    group = lane_group((HEADS, LANES), block_len)
    per_tile = LANES // block_len
    tiles = block_count // per_tile
    route_logs = []
    for route in range(route_count):
        parts = []
        for tile in range(tiles):
            gathered = jnp.zeros((HEADS, LANES), jnp.float32)
            for spot in range(per_tile):
                block = tile * per_tile + spot
                start = pl.multiple_of(routes[route, block] * HEADS, HEADS)
                shift = (spot + per_tile - ranks[route, block]) * block_len % LANES
                moved = pltpu.roll(logs[pl.ds(start, HEADS), :], shift, 1)
                gathered = jnp.where(group == spot, moved, gathered)
            parts.append(gathered)
        route_logs.append(jnp.concatenate(parts, axis=1))
    best = functools.reduce(jnp.maximum, route_logs)
    terms = [jnp.exp(item - best) for item in route_logs]
    total = functools.reduce(jnp.add, terms)
    spread = (
        lax.broadcasted_iota(jnp.int32, (2 * HEADS, width), 1) // (width // HEADS)
        == lax.broadcasted_iota(jnp.int32, (2 * HEADS, width), 0) % HEADS
    ).astype(jnp.float32).astype(jnp.bfloat16)
    weights = []
    for item in terms:
        share = item / total
        high = share.astype(jnp.bfloat16).astype(jnp.float32)
        both = jnp.concatenate([high, share - high], axis=0).astype(jnp.bfloat16)
        weights.append(mm_tn(both, spread))
    for block in range(block_count):
        rows = slice(block * block_len, (block + 1) * block_len)
        for pair in range(pairs):
            lanes = slice(pair * LANES, (pair + 1) * LANES)
            acc = None
            for route in range(route_count):
                start = pl.multiple_of(pair * pair_rows + ranks[route, block] * block_len, block_len)
                piece = back[routes[route, block], pl.ds(start, block_len), :].astype(jnp.float32)
                piece = piece * weights[route][rows, lanes]
                acc = piece if acc is None else acc + piece
            attended[rows, lanes] = acc.astype(jnp.bfloat16)


def own_kernel(head_scale, mesh, attended, w_out, w_qkv, encoded, query, keyval):
    width = attended.shape[1]
    rows = (mesh[...].astype(jnp.float32) + mm(attended[...], w_out[...])).astype(jnp.bfloat16)
    encoded[...] = rows
    qkv = mm(norm_rows(rows), w_qkv[...]).astype(jnp.bfloat16)
    query[...] = qkv[:, :width] * jnp.bfloat16(head_scale)
    keyval[...] = qkv[:, width:]


def window_kernel(edges, query, keyval, encoded, mesh_prev, mesh_next, att_prev, att_next, w_out, w_qkv, w_proc,
                  processed, mixed):
    rows, width = query.shape
    pairs = width // LANES
    mesh_both = jnp.concatenate([mesh_prev[...], mesh_next[...]], axis=0)
    att_both = jnp.concatenate([att_prev[...], att_next[...]], axis=0)
    near = (mesh_both.astype(jnp.float32) + mm(att_both, w_out[...])).astype(jnp.bfloat16)
    near_kv = mm(norm_rows(near), w_qkv[:, width:]).astype(jnp.bfloat16)
    query_pos = lax.broadcasted_iota(jnp.int32, (rows, rows), 0)
    key_pos = lax.broadcasted_iota(jnp.int32, (rows, rows), 1)
    before = jnp.where((key_pos >= query_pos) & (edges[0] > 0), 0.0, NEG)
    after = jnp.where((key_pos < query_pos) & (edges[1] > 0), 0.0, NEG)
    masks = half_masks()
    for pair in range(pairs):
        lanes = slice(pair * LANES, (pair + 1) * LANES)
        value_lanes = slice(width + pair * LANES, width + (pair + 1) * LANES)
        query_pair = query[:, lanes]
        key_parts = (near_kv[:rows, lanes], keyval[:, lanes], near_kv[rows:, lanes])
        value_all = jnp.concatenate(
            [near_kv[:rows, value_lanes], keyval[:, value_lanes], near_kv[rows:, value_lanes]], axis=0
        )
        mixed_pair = None
        for half in range(2):
            mask = masks[half]
            scores = [mm_nt(query_pair, part * mask) for part in key_parts]
            scores = [scores[0] + before, scores[1], scores[2] + after]
            top = jnp.max(jnp.maximum(jnp.maximum(scores[0], scores[1]), scores[2]), axis=-1, keepdims=True)
            terms = jnp.concatenate([jnp.exp(item - top).astype(jnp.bfloat16) for item in scores], axis=1)
            table = jnp.concatenate([value_all * mask, jnp.broadcast_to(mask, value_all.shape)], axis=1)
            product = mm(terms, table)
            mixed_pair = product if mixed_pair is None else mixed_pair + product
        mixed[:, lanes] = (mixed_pair[:, :LANES] / mixed_pair[:, LANES:]).astype(jnp.bfloat16)
    processed[...] = (encoded[...].astype(jnp.float32) + mm(mixed[...], w_proc[...])).astype(jnp.bfloat16)


def call(kernel, name, outs, in_specs, scratch, cost, out_specs=None, limit=40):
    return pl.pallas_call(
        kernel,
        name=name,
        out_shape=outs,
        in_specs=in_specs,
        out_specs=out_specs if out_specs is not None else [VMEM] * len(outs),
        scratch_shapes=scratch,
        cost_estimate=pl.CostEstimate(flops=cost[0], bytes_accessed=cost[1], transcendentals=cost[2]),
        compiler_params=pltpu.CompilerParams(vmem_limit_bytes=limit << 20),
    )


def shape(dims, dtype=jnp.bfloat16):
    return jax.ShapeDtypeStruct(dims, dtype)


def local(grid_feats, mesh_feats, routes, edge_first, edge_count, w_query, w_kv, w_out_enc, w_qkv, w_out_proc):
    width = w_query.shape[1]
    model = mesh_feats.shape[1]
    head_scale = 1.0 / math.sqrt(width // HEADS)
    node_count = lax.axis_size("outer") * lax.axis_size("inner")
    block_count, route_count = routes.shape
    rows = mesh_feats.shape[0]
    key_count = grid_feats.shape[0]
    block_len = rows // block_count
    capacity = max(1, (block_count * route_count + node_count - 1) // node_count)
    pairs = width // LANES
    pair_rows = capacity * block_len
    note_rows = max(8, -(-2 * capacity // 8) * 8)
    message = (node_count, pairs * pair_rows + note_rows, LANES)
    message_bytes = 2 * message[0] * message[1] * message[2]
    routes_t = routes.T
    place = (block_len, capacity)

    send, ranks = call(
        functools.partial(send_kernel, *place, head_scale),
        "send_queries",
        [shape(message), shape((route_count, block_count), jnp.int32)],
        [SMEM, VMEM, VMEM, VMEM, VMEM],
        [pltpu.SMEM((node_count,), jnp.int32), pltpu.VMEM((node_count * note_rows, LANES), jnp.float32)],
        (2 * rows * model * width, 2 * model * (rows + width) + message_bytes, 0),
        out_specs=[VMEM, SMEM],
    )(routes_t, edge_first.T, edge_count.T, mesh_feats, w_query)
    recv = lax.all_to_all(send, AXES, split_axis=0, concat_axis=0, tiled=True)

    keys, values = call(
        grid_kernel,
        "grid_keys",
        [shape((HEADS, key_count, LANES)), shape((pairs, 2 * key_count, 2 * LANES))],
        [VMEM, VMEM],
        [],
        (4 * key_count * model * width, 2 * model * (key_count + 2 * width) + 12 * key_count * width, 0),
    )(grid_feats, w_kv)

    forward = [(i, i + 1) for i in range(node_count - 1)]
    backward = [(i + 1, i) for i in range(node_count - 1)]
    late_mesh, keys = lax.optimization_barrier((mesh_feats, keys))
    mesh_prev = lax.ppermute(late_mesh, AXES, forward)
    mesh_next = lax.ppermute(late_mesh, AXES, backward)

    back = call(
        functools.partial(owner_kernel, *place),
        "owner_attention",
        [shape(message)],
        [VMEM, VMEM, VMEM],
        [pltpu.VMEM((node_count * pair_rows, key_count), jnp.float32)],
        (4 * node_count * pair_rows * key_count * width, 2 * message_bytes, node_count * pair_rows * key_count * HEADS),
    )(recv, keys, values)[0]
    back = lax.all_to_all(back, AXES, split_axis=0, concat_axis=0, tiled=True)

    attended = call(
        functools.partial(combine_kernel, *place),
        "combine_routes",
        [shape((rows, width))],
        [SMEM, SMEM, VMEM],
        [pltpu.VMEM((node_count * HEADS, LANES), jnp.float32)],
        (4 * rows * width * route_count, message_bytes, 0),
    )(routes_t, ranks, back)[0]
    att_prev = lax.ppermute(attended, AXES, forward)
    att_next = lax.ppermute(attended, AXES, backward)

    encoded, query, keyval = call(
        functools.partial(own_kernel, head_scale),
        "own_rows",
        [shape((rows, model)), shape((rows, width)), shape((rows, 2 * width))],
        [VMEM] * 4,
        [],
        (8 * rows * model * width, 2 * model * (2 * rows + 4 * width), 0),
    )(mesh_feats, attended, w_out_enc, w_qkv)

    place_index = lax.axis_index(AXES)
    edges = jnp.stack([place_index > 0, place_index < node_count - 1]).astype(jnp.int32)
    processed = call(
        window_kernel,
        "window_attention",
        [shape((rows, model))],
        [SMEM] + [VMEM] * 10,
        [pltpu.VMEM((rows, width), jnp.bfloat16)],
        (16 * rows * model * width, 2 * model * (4 * rows + 5 * width), 3 * rows * rows * HEADS),
    )(edges, query, keyval, encoded, mesh_prev, mesh_next, att_prev, att_next, w_out_enc, w_qkv, w_out_proc)[0]
    return (encoded, processed)


def solution(mesh):
    rows = P(("groups", "outer", "inner"), None)
    return jax.shard_map(
        local,
        mesh=mesh,
        in_specs=(rows,) * 5 + (P(),) * 5,
        out_specs=(rows, rows),
        check_vma=False,
    )
```

```python
import functools
import math

import jax
import jax.numpy as jnp
from jax import lax
from jax.experimental import pallas as pl
from jax.experimental.pallas import tpu as pltpu
from jax.sharding import PartitionSpec as P

HEADS = 8
WIN = 512
LANES = 128
NEG = -1e30
AXES = ("outer", "inner")
VMEM = pl.BlockSpec(memory_space=pltpu.VMEM)
SMEM = pl.BlockSpec(memory_space=pltpu.SMEM)
ANY = pl.BlockSpec(memory_space=pl.ANY)
HBM = pl.BlockSpec(memory_space=pltpu.HBM)
LIMIT = 50 << 20


def norm_rows(inputs):
    as_float = inputs.astype(jnp.float32)
    row_mean = jnp.mean(as_float, axis=-1, keepdims=True)
    centered = as_float - row_mean
    variance = jnp.mean(centered * centered, axis=-1, keepdims=True)
    return (centered * lax.rsqrt(variance + 1e-05)).astype(jnp.bfloat16)


def mm(a, b):
    return jnp.dot(a, b, preferred_element_type=jnp.float32)


def mm_nt(a, b):
    return lax.dot_general(a, b, (((1,), (1,)), ((), ())), preferred_element_type=jnp.float32)


def mm_tn(a, b):
    return lax.dot_general(a, b, (((0,), (0,)), ((), ())), preferred_element_type=jnp.float32)


def lane_group(shape, width):
    return lax.broadcasted_iota(jnp.int32, shape, len(shape) - 1) // width


def half_masks():
    low = (lane_group((1, LANES), LANES // 2) == 0).astype(jnp.float32)
    return low.astype(jnp.bfloat16), (1.0 - low).astype(jnp.bfloat16)


def fetch(pairs, sems):
    copies = [pltpu.make_async_copy(src, dst, sems.at[i]) for i, (src, dst) in enumerate(pairs)]
    for item in copies:
        item.start()
    return copies


def send_kernel(block_len, capacity, query_scale, routes_h, first_h, count_h, mesh_h, w_query_h, send, ranks,
                routes, first, count, mesh, w_query, tally, notes, sems):
    copies = fetch(
        [(mesh_h, mesh), (w_query_h, w_query), (routes_h, routes), (first_h, first), (count_h, count)], sems
    )
    route_count, block_count = routes.shape
    node_count = send.shape[0]
    pair_rows = capacity * block_len
    pairs = w_query.shape[1] // LANES
    note_rows = send.shape[1] - pairs * pair_rows

    def clear(i, carry):
        tally[i] = 0
        return carry

    lax.fori_loop(0, node_count, clear, 0)
    if node_count * capacity != block_count * route_count:
        send[...] = jnp.zeros(send.shape, send.dtype)
    notes[...] = jnp.zeros(notes.shape, notes.dtype)
    copies[0].wait()
    normed = norm_rows(mesh[...])
    for item in copies[1:]:
        item.wait()
    first_all = first[...]
    upper = first_all >= 256
    low_part = jnp.where(upper, first_all - 256, first_all).astype(jnp.float32)
    signed = jnp.where(upper, -count[...], count[...]).astype(jnp.float32)
    group = lane_group((1, LANES), block_len)
    per_tile = LANES // block_len
    queries = (mm(normed, w_query[...]) * query_scale).astype(jnp.bfloat16)
    for block in range(block_count):
        tile, spot = divmod(block, per_tile)
        cols = slice(tile * LANES, (tile + 1) * LANES)
        rows = slice(block * block_len, (block + 1) * block_len)
        for route in range(route_count):
            owner = routes[route, block]
            rank = tally[owner]
            tally[owner] = rank + 1
            ranks[route, block] = rank
            for pair in range(pairs):
                start = pl.multiple_of(pair * pair_rows + rank * block_len, block_len)
                send[owner, pl.ds(start, block_len), :] = queries[rows, pair * LANES:(pair + 1) * LANES]
            note = owner * note_rows + 2 * rank
            keep = group == spot
            notes[pl.ds(note, 1), :] = jnp.where(keep, low_part[route:route + 1, cols], 0.0)
            notes[pl.ds(note + 1, 1), :] = jnp.where(keep, signed[route:route + 1, cols], 0.0)
    for owner in range(node_count):
        send[owner, pairs * pair_rows:, :] = notes[owner * note_rows:(owner + 1) * note_rows, :].astype(jnp.bfloat16)


def grid_kernel(grid_h, w_kv_h, table, grid, w_kv, sems):
    copies = fetch([(grid_h, grid), (w_kv_h, w_kv)], sems)
    width = w_kv.shape[1] // 2
    copies[0].wait()
    normed = norm_rows(grid[...])
    copies[1].wait()
    grid_kv = mm(normed, w_kv[...]).astype(jnp.bfloat16)
    count = grid_kv.shape[0]
    masks = half_masks()
    for pair in range(width // LANES):
        key_pair = grid_kv[:, pair * LANES:(pair + 1) * LANES]
        value_pair = grid_kv[:, width + pair * LANES:width + (pair + 1) * LANES]
        for half in range(2):
            mask = masks[half]
            rows = slice(half * count, (half + 1) * count)
            table[pair, rows, :LANES] = value_pair * mask
            table[pair, rows, LANES:] = jnp.broadcast_to(mask, (count, LANES))
            table[pair, 2 * count:, half * LANES:(half + 1) * LANES] = key_pair * mask


def owner_kernel(block_len, capacity, chunk, recv_h, table_h, back_h, recv, table, back, bias, sems, outs):
    node_count, message_rows, _ = recv.shape
    pairs, table_rows, _ = table.shape
    key_count = table_rows // 3
    pair_rows = capacity * block_len
    note_rows = message_rows - pairs * pair_rows
    row_count = node_count * pair_rows
    group = chunk // pair_rows
    chunks = row_count // chunk
    copies = fetch([(recv_h, recv), (table_h, table)], sems)
    copies[0].wait()
    tags = recv[:, pairs * pair_rows:, :].reshape(node_count * note_rows, LANES)
    fold = (
        lax.broadcasted_iota(jnp.int32, (block_len, LANES), 1) % block_len
        == lax.broadcasted_iota(jnp.int32, (block_len, LANES), 0)
    ).astype(jnp.float32).astype(jnp.bfloat16)
    columns = mm_nt(fold, tags)
    key_pos = lax.broadcasted_iota(jnp.int32, (block_len, key_count), 1).astype(jnp.float32)
    for owner in range(node_count):
        for rank in range(capacity):
            spot = owner * note_rows + 2 * rank
            low_part, signed = columns[:, spot:spot + 1], columns[:, spot + 1:spot + 2]
            begin = low_part + jnp.where(signed < 0, 256.0, 0.0)
            end = begin + jnp.maximum(jnp.abs(signed), 1.0)
            inside = (key_pos >= begin) & (key_pos < end)
            row = (owner * capacity + rank) * block_len
            bias[row:row + block_len, :] = jnp.where(inside, 0.0, NEG)
    copies[1].wait()
    low_half = lane_group((chunk, LANES), LANES // 2) == 0
    pick_row = lax.broadcasted_iota(jnp.int32, (HEADS, LANES), 0)
    pick_lane = lax.broadcasted_iota(jnp.int32, (HEADS, LANES), 1)
    half_lane = lane_group((HEADS, LANES), LANES // 2)

    def step(index, carry):
        span = pl.ds(index * group, group)
        mask = bias[pl.ds(pl.multiple_of(index * chunk, chunk), chunk), :]
        log_high = jnp.zeros((HEADS, chunk), jnp.float32)
        log_low = jnp.zeros((HEADS, chunk), jnp.float32)
        scores, softs, mixes = {}, {}, {}
        for turn in range(HEADS + 4):
            if turn < HEADS:
                pair = turn // 2
                rows = recv[span, pair * pair_rows:(pair + 1) * pair_rows, :].reshape(chunk, LANES)
                half = turn % 2
                scores[turn] = mm_nt(rows, table[pair, 2 * key_count:, half * LANES:(half + 1) * LANES]) + mask
            head = turn - 2
            if 0 <= head < HEADS:
                item = scores.pop(head)
                top = jnp.max(item, axis=-1, keepdims=True)
                softs[head] = (top, jnp.exp2(item - top).astype(jnp.bfloat16))
            head = turn - 4
            if head < 0:
                continue
            pair, half = divmod(head, 2)
            mixes[head] = mm(softs[head][1], table[pair, half * key_count:(half + 1) * key_count, :])
            if half == 0:
                continue
            mixed = mixes.pop(head - 1) + mixes.pop(head)
            total = mixed[:, LANES:]
            part = slice(pair * pair_rows, (pair + 1) * pair_rows)
            back[span, part, :] = (mixed[:, :LANES] / total).astype(jnp.bfloat16).reshape(group, pair_rows, LANES)
            logs = jnp.where(low_half, softs.pop(head - 1)[0], softs.pop(head)[0]) + jnp.log2(total)
            high = logs.astype(jnp.bfloat16)
            low = (logs - high.astype(jnp.float32)).astype(jnp.bfloat16)
            pick = (
                ((pick_row == 2 * pair) & (pick_lane == 0)) | ((pick_row == 2 * pair + 1) & (pick_lane == LANES // 2))
            ).astype(jnp.float32).astype(jnp.bfloat16)
            log_high = log_high + mm_nt(pick, high)
            log_low = log_low + mm_nt(pick, low)
        for offset in range(group):
            lane = offset * pair_rows
            tile, shift = lane // LANES, lane % LANES
            high = log_high[:, tile * LANES:(tile + 1) * LANES]
            low = log_low[:, tile * LANES:(tile + 1) * LANES]
            if shift:
                high = pltpu.roll(high, LANES - shift, 1)
            low_shift = (LANES // 2 - shift) % LANES
            if low_shift:
                low = pltpu.roll(low, low_shift, 1)
            back[index * group + offset, pairs * pair_rows:pairs * pair_rows + HEADS, :] = jnp.where(
                half_lane == 0, high, low
            ).astype(jnp.bfloat16)
        pltpu.make_async_copy(back.at[span], back_h.at[span], outs.at[index]).start()
        return carry

    lax.fori_loop(0, chunks, step, 0)
    for index in range(chunks):
        span = pl.ds(index * group, group)
        pltpu.make_async_copy(back.at[span], back_h.at[span], outs.at[index]).wait()


def combine_kernel(block_len, capacity, routes_h, ranks_h, back_h, attended, routes, ranks, back, logs, sems):
    node_count, message_rows, _ = back.shape
    width = attended.shape[1]
    pairs = width // LANES
    pair_rows = capacity * block_len
    copies = fetch(
        [
            (routes_h, routes),
            (ranks_h, ranks),
            (back_h.at[:, pl.ds(pairs * pair_rows, HEADS)], back.at[:, pl.ds(pairs * pair_rows, HEADS)]),
            (back_h.at[:, pl.ds(0, pairs * pair_rows)], back.at[:, pl.ds(0, pairs * pair_rows)]),
        ],
        sems,
    )
    route_count, block_count = routes.shape
    for item in copies[:3]:
        item.wait()
    halves = back[:, pairs * pair_rows:pairs * pair_rows + HEADS, :].astype(jnp.float32).reshape(node_count * HEADS, LANES)
    logs[...] = halves + pltpu.roll(halves, LANES // 2, 1)
    group = lane_group((HEADS, LANES), block_len)
    per_tile = LANES // block_len
    tiles = block_count // per_tile
    route_logs = []
    for route in range(route_count):
        parts = []
        for tile in range(tiles):
            gathered = jnp.zeros((HEADS, LANES), jnp.float32)
            for spot in range(per_tile):
                block = tile * per_tile + spot
                start = pl.multiple_of(routes[route, block] * HEADS, HEADS)
                shift = (spot + per_tile - ranks[route, block]) * block_len % LANES
                moved = pltpu.roll(logs[pl.ds(start, HEADS), :], shift, 1)
                gathered = jnp.where(group == spot, moved, gathered)
            parts.append(gathered)
        route_logs.append(jnp.concatenate(parts, axis=1))
    best = functools.reduce(jnp.maximum, route_logs)
    terms = [jnp.exp2(item - best) for item in route_logs]
    total = functools.reduce(jnp.add, terms)
    spread = (
        lax.broadcasted_iota(jnp.int32, (2 * HEADS, width), 1) // (width // HEADS)
        == lax.broadcasted_iota(jnp.int32, (2 * HEADS, width), 0) % HEADS
    ).astype(jnp.float32).astype(jnp.bfloat16)
    weights = []
    for item in terms:
        share = item / total
        high = share.astype(jnp.bfloat16).astype(jnp.float32)
        both = jnp.concatenate([high, share - high], axis=0).astype(jnp.bfloat16)
        weights.append(mm_tn(both, spread))
    copies[3].wait()
    for block in range(block_count):
        rows = slice(block * block_len, (block + 1) * block_len)
        for pair in range(pairs):
            lanes = slice(pair * LANES, (pair + 1) * LANES)
            acc = None
            for route in range(route_count):
                start = pl.multiple_of(pair * pair_rows + ranks[route, block] * block_len, block_len)
                piece = back[routes[route, block], pl.ds(start, block_len), :].astype(jnp.float32)
                piece = piece * weights[route][rows, lanes]
                acc = piece if acc is None else acc + piece
            attended[rows, lanes] = acc.astype(jnp.bfloat16)


def own_kernel(query_scale, mesh_h, attended_h, w_out_h, w_qkv_h, encoded, own, mesh, attended, w_out, w_qkv, sems):
    copies = fetch([(attended_h, attended), (w_out_h, w_out), (mesh_h, mesh), (w_qkv_h, w_qkv)], sems)
    width = attended.shape[1]
    for item in copies[:3]:
        item.wait()
    rows = (mesh[...].astype(jnp.float32) + mm(attended[...], w_out[...])).astype(jnp.bfloat16)
    encoded[...] = rows
    own[:, 3 * width:] = rows
    normed = norm_rows(rows)
    copies[3].wait()
    own[:, :width] = (mm(normed, w_qkv[:, :width]) * query_scale).astype(jnp.bfloat16)
    own[:, width:3 * width] = mm(normed, w_qkv[:, width:]).astype(jnp.bfloat16)


def window_kernel(edges, own_h, mesh_prev_h, mesh_next_h, att_prev_h, att_next_h, w_out_h, w_qkv_h, w_proc_h,
                  processed, own, mesh_both, att_both, w_out, w_near, w_proc, mixed, sems):
    rows, width = mixed.shape
    pairs = width // LANES
    upper, lower = pl.ds(0, rows), pl.ds(rows, rows)
    copies = fetch(
        [
            (att_prev_h, att_both.at[upper]),
            (att_next_h, att_both.at[lower]),
            (w_out_h, w_out),
            (mesh_prev_h, mesh_both.at[upper]),
            (mesh_next_h, mesh_both.at[lower]),
            (w_qkv_h.at[:, pl.ds(width, 2 * width)], w_near),
            (own_h, own),
            (w_proc_h, w_proc),
        ],
        sems,
    )
    for item in copies[:5]:
        item.wait()
    near = (mesh_both[...].astype(jnp.float32) + mm(att_both[...], w_out[...])).astype(jnp.bfloat16)
    normed = norm_rows(near)
    for item in copies[5:]:
        item.wait()
    near_kv = mm(normed, w_near[...]).astype(jnp.bfloat16)
    query_pos = lax.broadcasted_iota(jnp.int32, (rows, rows), 0)
    key_pos = lax.broadcasted_iota(jnp.int32, (rows, rows), 1)
    before = jnp.where((key_pos >= query_pos) & (edges[0] > 0), 0.0, NEG)
    after = jnp.where((key_pos < query_pos) & (edges[1] > 0), 0.0, NEG)
    masks = half_masks()
    for pair in range(pairs):
        lanes = slice(pair * LANES, (pair + 1) * LANES)
        value_lanes = slice(width + pair * LANES, width + (pair + 1) * LANES)
        query_pair = own[:, lanes]
        own_keys = own[:, width + pair * LANES:width + (pair + 1) * LANES]
        own_values = own[:, 2 * width + pair * LANES:2 * width + (pair + 1) * LANES]
        key_parts = (near_kv[:rows, lanes], own_keys, near_kv[rows:, lanes])
        value_all = jnp.concatenate([near_kv[:rows, value_lanes], own_values, near_kv[rows:, value_lanes]], axis=0)
        mixed_pair = None
        for half in range(2):
            mask = masks[half]
            scores = [mm_nt(query_pair, part * mask) for part in key_parts]
            scores = [scores[0] + before, scores[1], scores[2] + after]
            top = jnp.max(jnp.maximum(jnp.maximum(scores[0], scores[1]), scores[2]), axis=-1, keepdims=True)
            terms = jnp.concatenate([jnp.exp2(item - top).astype(jnp.bfloat16) for item in scores], axis=1)
            table = jnp.concatenate([value_all * mask, jnp.broadcast_to(mask, value_all.shape)], axis=1)
            product = mm(terms, table)
            mixed_pair = product if mixed_pair is None else mixed_pair + product
        mixed[:, lanes] = (mixed_pair[:, :LANES] / mixed_pair[:, LANES:]).astype(jnp.bfloat16)
    processed[...] = (own[:, 3 * width:].astype(jnp.float32) + mm(mixed[...], w_proc[...])).astype(jnp.bfloat16)


def call(kernel, name, outs, out_specs, operands, scratch, cost, limit=LIMIT):
    return pl.pallas_call(
        kernel,
        name=name,
        out_shape=outs,
        in_specs=[SMEM if item.shape == (2,) else ANY for item in operands],
        out_specs=out_specs,
        scratch_shapes=scratch,
        cost_estimate=pl.CostEstimate(flops=cost[0], bytes_accessed=cost[1], transcendentals=cost[2]),
        compiler_params=pltpu.CompilerParams(vmem_limit_bytes=limit),
    )(*operands)


def shape(dims, dtype=jnp.bfloat16):
    return jax.ShapeDtypeStruct(dims, dtype)


def held(item):
    return pltpu.VMEM(item.shape, item.dtype)


def dma(count):
    return pltpu.SemaphoreType.DMA((count,))


def local(grid_feats, mesh_feats, routes, edge_first, edge_count, w_query, w_kv, w_out_enc, w_qkv, w_out_proc):
    width = w_query.shape[1]
    model = mesh_feats.shape[1]
    query_scale = math.log2(math.e) / math.sqrt(width // HEADS)
    node_count = lax.axis_size("outer") * lax.axis_size("inner")
    block_count, route_count = routes.shape
    rows = mesh_feats.shape[0]
    key_count = grid_feats.shape[0]
    block_len = rows // block_count
    capacity = max(1, (block_count * route_count + node_count - 1) // node_count)
    pairs = width // LANES
    pair_rows = capacity * block_len
    note_rows = max(8, -(-2 * capacity // 8) * 8)
    message = shape((node_count, pairs * pair_rows + note_rows, LANES))
    message_bytes = 2 * math.prod(message.shape)
    routes_t, first_t, count_t = routes.T, edge_first.T, edge_count.T
    ranks_shape = shape(routes_t.shape, jnp.int32)
    in_smem = pltpu.SMEM(routes_t.shape, jnp.int32)
    place = (block_len, capacity)

    send, ranks = call(
        functools.partial(send_kernel, *place, query_scale),
        "send_queries",
        [message, ranks_shape],
        [VMEM, SMEM],
        (routes_t, first_t, count_t, mesh_feats, w_query),
        [in_smem, held(first_t), held(count_t), held(mesh_feats), held(w_query), pltpu.SMEM((node_count,), jnp.int32),
         pltpu.VMEM((node_count * note_rows, LANES), jnp.float32), dma(5)],
        (2 * rows * model * width, 2 * model * (rows + width) + message_bytes, 0),
        None,
    )
    recv = lax.all_to_all(send, AXES, split_axis=0, concat_axis=0, tiled=True)

    table = call(
        grid_kernel,
        "grid_keys",
        shape((pairs, 3 * key_count, 2 * LANES)),
        VMEM,
        (grid_feats, w_kv),
        [held(grid_feats), held(w_kv), dma(2)],
        (4 * key_count * model * width, 2 * model * (key_count + 2 * width) + 12 * key_count * width, 0),
        None,
    )

    forward = [(i, i + 1) for i in range(node_count - 1)]
    backward = [(i + 1, i) for i in range(node_count - 1)]
    late_mesh, table = lax.optimization_barrier((mesh_feats, table))
    mesh_prev = lax.ppermute(late_mesh, AXES, forward)
    mesh_next = lax.ppermute(late_mesh, AXES, backward)

    chunk = math.gcd(node_count * pair_rows, 512)
    back = call(
        functools.partial(owner_kernel, *place, chunk),
        "owner_attention",
        message,
        HBM,
        (recv, table),
        [held(message), held(table), held(message),
         pltpu.VMEM((node_count * pair_rows, key_count), jnp.float32), dma(2), dma(node_count * pair_rows // chunk)],
        (4 * node_count * pair_rows * key_count * width, 2 * message_bytes, node_count * pair_rows * key_count * HEADS),
    )
    back = lax.all_to_all(back, AXES, split_axis=0, concat_axis=0, tiled=True)

    attended = call(
        functools.partial(combine_kernel, *place),
        "combine_routes",
        shape((rows, width)),
        VMEM,
        (routes_t, ranks, back),
        [in_smem, in_smem, held(message), pltpu.VMEM((node_count * HEADS, LANES), jnp.float32), dma(4)],
        (4 * rows * width * route_count, message_bytes, 0),
    )
    att_prev = lax.ppermute(attended, AXES, forward)
    att_next = lax.ppermute(attended, AXES, backward)

    encoded, own = call(
        functools.partial(own_kernel, query_scale),
        "own_rows",
        [shape((rows, model)), shape((rows, 3 * width + model))],
        [VMEM] * 2,
        (mesh_feats, attended, w_out_enc, w_qkv),
        [held(mesh_feats), held(attended), held(w_out_enc), held(w_qkv), dma(4)],
        (8 * rows * model * width, 2 * model * (2 * rows + 4 * width), 0),
    )

    place_index = lax.axis_index(AXES)
    edges = jnp.stack([place_index > 0, place_index < node_count - 1]).astype(jnp.int32)
    processed = call(
        window_kernel,
        "window_attention",
        shape((rows, model)),
        VMEM,
        (edges, own, mesh_prev, mesh_next, att_prev, att_next, w_out_enc, w_qkv, w_out_proc),
        [held(own), pltpu.VMEM((2 * rows, model), jnp.bfloat16),
         pltpu.VMEM((2 * rows, width), jnp.bfloat16), held(w_out_enc), pltpu.VMEM((model, 2 * width), jnp.bfloat16),
         held(w_out_proc), pltpu.VMEM((rows, width), jnp.bfloat16), dma(8)],
        (16 * rows * model * width, 2 * model * (4 * rows + 5 * width), 3 * rows * rows * HEADS),
    )
    return (encoded, processed)


def solution(mesh):
    rows = P(("groups", "outer", "inner"), None)
    return jax.shard_map(
        local,
        mesh=mesh,
        in_specs=(rows,) * 5 + (P(),) * 5,
        out_specs=(rows, rows),
        check_vma=False,
    )
```

```python
import functools
import math

import jax
import jax.numpy as jnp
from jax import lax
from jax.experimental import pallas as pl
from jax.experimental.pallas import tpu as pltpu
from jax.sharding import PartitionSpec as P

HEADS = 8
WIN = 512
LANES = 128
NEG = -1e30
AXES = ("outer", "inner")
VMEM = pl.BlockSpec(memory_space=pltpu.VMEM)
SMEM = pl.BlockSpec(memory_space=pltpu.SMEM)
ANY = pl.BlockSpec(memory_space=pl.ANY)
HBM = pl.BlockSpec(memory_space=pltpu.HBM)
LIMIT = 50 << 20


def norm_rows(inputs):
    as_float = inputs.astype(jnp.float32)
    row_mean = jnp.mean(as_float, axis=-1, keepdims=True)
    centered = as_float - row_mean
    variance = jnp.mean(centered * centered, axis=-1, keepdims=True)
    return (centered * lax.rsqrt(variance + 1e-05)).astype(jnp.bfloat16)


def mm(a, b):
    return jnp.dot(a, b, preferred_element_type=jnp.float32)


def mm_nt(a, b):
    return lax.dot_general(a, b, (((1,), (1,)), ((), ())), preferred_element_type=jnp.float32)


def mm_tn(a, b):
    return lax.dot_general(a, b, (((0,), (0,)), ((), ())), preferred_element_type=jnp.float32)


def lane_group(shape, width):
    return lax.broadcasted_iota(jnp.int32, shape, len(shape) - 1) // width


def half_masks():
    low = (lane_group((1, LANES), LANES // 2) == 0).astype(jnp.float32)
    return low.astype(jnp.bfloat16), (1.0 - low).astype(jnp.bfloat16)


def fetch(pairs, sems):
    copies = [pltpu.make_async_copy(src, dst, sems.at[i]) for i, (src, dst) in enumerate(pairs)]
    for item in copies:
        item.start()
    return copies


def send_kernel(block_len, capacity, query_scale, routes_h, first_h, count_h, mesh_h, w_query_h, send, ranks,
                routes, first, count, mesh, w_query, tally, notes, sems):
    copies = fetch(
        [(mesh_h, mesh), (w_query_h, w_query), (routes_h, routes), (first_h, first), (count_h, count)], sems
    )
    route_count, block_count = routes.shape
    node_count = send.shape[0]
    pair_rows = capacity * block_len
    pairs = w_query.shape[1] // LANES
    note_rows = send.shape[1] - pairs * pair_rows

    def clear(i, carry):
        tally[i] = 0
        return carry

    lax.fori_loop(0, node_count, clear, 0)
    if node_count * capacity != block_count * route_count:
        send[...] = jnp.zeros(send.shape, send.dtype)
    notes[...] = jnp.zeros(notes.shape, notes.dtype)
    copies[0].wait()
    normed = norm_rows(mesh[...])
    for item in copies[1:]:
        item.wait()
    first_all = first[...]
    upper = first_all >= 256
    low_part = jnp.where(upper, first_all - 256, first_all).astype(jnp.float32)
    signed = jnp.where(upper, -count[...], count[...]).astype(jnp.float32)
    group = lane_group((1, LANES), block_len)
    per_tile = LANES // block_len
    queries = (mm(normed, w_query[...]) * query_scale).astype(jnp.bfloat16)
    for block in range(block_count):
        tile, spot = divmod(block, per_tile)
        cols = slice(tile * LANES, (tile + 1) * LANES)
        rows = slice(block * block_len, (block + 1) * block_len)
        for route in range(route_count):
            owner = routes[route, block]
            rank = tally[owner]
            tally[owner] = rank + 1
            ranks[route, block] = rank
            for pair in range(pairs):
                start = pl.multiple_of(pair * pair_rows + rank * block_len, block_len)
                send[owner, pl.ds(start, block_len), :] = queries[rows, pair * LANES:(pair + 1) * LANES]
            note = owner * note_rows + 2 * rank
            keep = group == spot
            notes[pl.ds(note, 1), :] = jnp.where(keep, low_part[route:route + 1, cols], 0.0)
            notes[pl.ds(note + 1, 1), :] = jnp.where(keep, signed[route:route + 1, cols], 0.0)
    for owner in range(node_count):
        send[owner, pairs * pair_rows:, :] = notes[owner * note_rows:(owner + 1) * note_rows, :].astype(jnp.bfloat16)


def grid_kernel(grid_h, w_kv_h, table, grid, w_kv, sems):
    copies = fetch([(grid_h, grid), (w_kv_h, w_kv)], sems)
    width = w_kv.shape[1] // 2
    copies[0].wait()
    normed = norm_rows(grid[...])
    copies[1].wait()
    grid_kv = mm(normed, w_kv[...]).astype(jnp.bfloat16)
    count = grid_kv.shape[0]
    masks = half_masks()
    for pair in range(width // LANES):
        key_pair = grid_kv[:, pair * LANES:(pair + 1) * LANES]
        value_pair = grid_kv[:, width + pair * LANES:width + (pair + 1) * LANES]
        for half in range(2):
            mask = masks[half]
            rows = slice(half * count, (half + 1) * count)
            table[pair, rows, :LANES] = value_pair * mask
            table[pair, rows, LANES:] = jnp.broadcast_to(mask, (count, LANES))
            table[pair, 2 * count:, half * LANES:(half + 1) * LANES] = key_pair * mask


def owner_kernel(block_len, capacity, chunk, recv_h, table_h, back_h, recv, table, back, bias, sems, outs):
    node_count, message_rows, _ = recv.shape
    pairs, table_rows, _ = table.shape
    key_count = table_rows // 3
    pair_rows = capacity * block_len
    note_rows = message_rows - pairs * pair_rows
    row_count = node_count * pair_rows
    group = chunk // pair_rows
    chunks = row_count // chunk
    copies = fetch([(recv_h, recv), (table_h, table)], sems)
    copies[0].wait()
    tags = recv[:, pairs * pair_rows:, :].reshape(node_count * note_rows, LANES)
    fold = (
        lax.broadcasted_iota(jnp.int32, (block_len, LANES), 1) % block_len
        == lax.broadcasted_iota(jnp.int32, (block_len, LANES), 0)
    ).astype(jnp.float32).astype(jnp.bfloat16)
    columns = mm_nt(fold, tags)
    key_pos = lax.broadcasted_iota(jnp.int32, (block_len, key_count), 1).astype(jnp.float32)
    for owner in range(node_count):
        for rank in range(capacity):
            spot = owner * note_rows + 2 * rank
            low_part, signed = columns[:, spot:spot + 1], columns[:, spot + 1:spot + 2]
            begin = low_part + jnp.where(signed < 0, 256.0, 0.0)
            end = begin + jnp.maximum(jnp.abs(signed), 1.0)
            inside = (key_pos >= begin) & (key_pos < end)
            row = (owner * capacity + rank) * block_len
            bias[row:row + block_len, :] = jnp.where(inside, 0.0, NEG)
    copies[1].wait()
    low_half = lane_group((chunk, LANES), LANES // 2) == 0
    pick_row = lax.broadcasted_iota(jnp.int32, (HEADS, LANES), 0)
    pick_lane = lax.broadcasted_iota(jnp.int32, (HEADS, LANES), 1)
    half_lane = lane_group((HEADS, LANES), LANES // 2)

    def step(index, carry):
        span = pl.ds(index * group, group)
        mask = bias[pl.ds(pl.multiple_of(index * chunk, chunk), chunk), :]
        log_high = jnp.zeros((HEADS, chunk), jnp.float32)
        log_low = jnp.zeros((HEADS, chunk), jnp.float32)
        scores, softs, mixes = {}, {}, {}
        for turn in range(HEADS + 4):
            if turn < HEADS:
                pair = turn // 2
                rows = recv[span, pair * pair_rows:(pair + 1) * pair_rows, :].reshape(chunk, LANES)
                half = turn % 2
                scores[turn] = mm_nt(rows, table[pair, 2 * key_count:, half * LANES:(half + 1) * LANES]) + mask
            head = turn - 2
            if 0 <= head < HEADS:
                item = scores.pop(head)
                top = jnp.max(item, axis=-1, keepdims=True)
                softs[head] = (top, jnp.exp2(item - top).astype(jnp.bfloat16))
            head = turn - 4
            if head < 0:
                continue
            pair, half = divmod(head, 2)
            mixes[head] = mm(softs[head][1], table[pair, half * key_count:(half + 1) * key_count, :])
            if half == 0:
                continue
            mixed = mixes.pop(head - 1) + mixes.pop(head)
            total = mixed[:, LANES:]
            part = slice(pair * pair_rows, (pair + 1) * pair_rows)
            back[span, part, :] = (mixed[:, :LANES] / total).astype(jnp.bfloat16).reshape(group, pair_rows, LANES)
            logs = jnp.where(low_half, softs.pop(head - 1)[0], softs.pop(head)[0]) + jnp.log2(total)
            high = logs.astype(jnp.bfloat16)
            low = (logs - high.astype(jnp.float32)).astype(jnp.bfloat16)
            pick = (
                ((pick_row == 2 * pair) & (pick_lane == 0)) | ((pick_row == 2 * pair + 1) & (pick_lane == LANES // 2))
            ).astype(jnp.float32).astype(jnp.bfloat16)
            log_high = log_high + mm_nt(pick, high)
            log_low = log_low + mm_nt(pick, low)
        for offset in range(group):
            lane = offset * pair_rows
            tile, shift = lane // LANES, lane % LANES
            high = log_high[:, tile * LANES:(tile + 1) * LANES]
            low = log_low[:, tile * LANES:(tile + 1) * LANES]
            if shift:
                high = pltpu.roll(high, LANES - shift, 1)
            low_shift = (LANES // 2 - shift) % LANES
            if low_shift:
                low = pltpu.roll(low, low_shift, 1)
            back[index * group + offset, pairs * pair_rows:pairs * pair_rows + HEADS, :] = jnp.where(
                half_lane == 0, high, low
            ).astype(jnp.bfloat16)
        pltpu.make_async_copy(back.at[span], back_h.at[span], outs.at[index]).start()
        return carry

    lax.fori_loop(0, chunks, step, 0)
    for index in range(chunks):
        span = pl.ds(index * group, group)
        pltpu.make_async_copy(back.at[span], back_h.at[span], outs.at[index]).wait()


def combine_kernel(block_len, capacity, routes_h, ranks_h, back_h, attended, routes, ranks, back, logs, sems):
    node_count, message_rows, _ = back.shape
    width = attended.shape[1]
    pairs = width // LANES
    pair_rows = capacity * block_len
    copies = fetch(
        [
            (routes_h, routes),
            (ranks_h, ranks),
            (back_h.at[:, pl.ds(pairs * pair_rows, HEADS)], back.at[:, pl.ds(pairs * pair_rows, HEADS)]),
            (back_h.at[:, pl.ds(0, pairs * pair_rows)], back.at[:, pl.ds(0, pairs * pair_rows)]),
        ],
        sems,
    )
    route_count, block_count = routes.shape
    for item in copies[:3]:
        item.wait()
    halves = back[:, pairs * pair_rows:pairs * pair_rows + HEADS, :].astype(jnp.float32).reshape(node_count * HEADS, LANES)
    logs[...] = halves + pltpu.roll(halves, LANES // 2, 1)
    group = lane_group((HEADS, LANES), block_len)
    per_tile = LANES // block_len
    tiles = block_count // per_tile
    route_logs = []
    for route in range(route_count):
        parts = []
        for tile in range(tiles):
            gathered = jnp.zeros((HEADS, LANES), jnp.float32)
            for spot in range(per_tile):
                block = tile * per_tile + spot
                start = pl.multiple_of(routes[route, block] * HEADS, HEADS)
                shift = (spot + per_tile - ranks[route, block]) * block_len % LANES
                moved = pltpu.roll(logs[pl.ds(start, HEADS), :], shift, 1)
                gathered = jnp.where(group == spot, moved, gathered)
            parts.append(gathered)
        route_logs.append(jnp.concatenate(parts, axis=1))
    best = functools.reduce(jnp.maximum, route_logs)
    terms = [jnp.exp2(item - best) for item in route_logs]
    total = functools.reduce(jnp.add, terms)
    spread = (
        lax.broadcasted_iota(jnp.int32, (2 * HEADS, width), 1) // (width // HEADS)
        == lax.broadcasted_iota(jnp.int32, (2 * HEADS, width), 0) % HEADS
    ).astype(jnp.float32).astype(jnp.bfloat16)
    weights = []
    for item in terms:
        share = item / total
        high = share.astype(jnp.bfloat16).astype(jnp.float32)
        both = jnp.concatenate([high, share - high], axis=0).astype(jnp.bfloat16)
        weights.append(mm_tn(both, spread))
    copies[3].wait()
    for block in range(block_count):
        rows = slice(block * block_len, (block + 1) * block_len)
        for pair in range(pairs):
            lanes = slice(pair * LANES, (pair + 1) * LANES)
            acc = None
            for route in range(route_count):
                start = pl.multiple_of(pair * pair_rows + ranks[route, block] * block_len, block_len)
                piece = back[routes[route, block], pl.ds(start, block_len), :].astype(jnp.float32)
                piece = piece * weights[route][rows, lanes]
                acc = piece if acc is None else acc + piece
            attended[rows, lanes] = acc.astype(jnp.bfloat16)


def own_kernel(query_scale, mesh_h, attended_h, w_out_h, w_qkv_h, encoded, own, mixes, tops,
               mesh, attended, w_out, w_qkv, sems):
    copies = fetch([(attended_h, attended), (w_out_h, w_out), (mesh_h, mesh), (w_qkv_h, w_qkv)], sems)
    width = attended.shape[1]
    for item in copies[:3]:
        item.wait()
    rows = (mesh[...].astype(jnp.float32) + mm(attended[...], w_out[...])).astype(jnp.bfloat16)
    encoded[...] = rows
    own[:, width:] = rows
    normed = norm_rows(rows)
    copies[3].wait()
    query = (mm(normed, w_qkv[:, :width]) * query_scale).astype(jnp.bfloat16)
    own[:, :width] = query
    keyval = mm(normed, w_qkv[:, width:]).astype(jnp.bfloat16)
    low_half = lane_group((rows.shape[0], LANES), LANES // 2) == 0
    masks = half_masks()
    scores, softs, mixed = {}, {}, {}
    for turn in range(HEADS + 2):
        if turn < HEADS:
            lanes = slice(turn // 2 * LANES, (turn // 2 + 1) * LANES)
            scores[turn] = mm_nt(query[:, lanes], keyval[:, lanes] * masks[turn % 2])
        head = turn - 1
        if 0 <= head < HEADS:
            item = scores.pop(head)
            top = jnp.max(item, axis=-1, keepdims=True)
            softs[head] = (top, jnp.exp2(item - top).astype(jnp.bfloat16))
        head = turn - 2
        if head < 0:
            continue
        pair, half = divmod(head, 2)
        value = keyval[:, width + pair * LANES:width + (pair + 1) * LANES]
        table = jnp.concatenate([value * masks[half], jnp.broadcast_to(masks[half], value.shape)], axis=1)
        mixed[half] = mm(softs[head][1], table)
        if half:
            mixes[pair] = mixed[0] + mixed[1]
            tops[pair] = jnp.where(low_half, softs.pop(head - 1)[0], softs.pop(head)[0])


def window_kernel(edges, own_h, mixes_h, tops_h, mesh_prev_h, mesh_next_h, att_prev_h, att_next_h, w_out_h, w_qkv_h,
                  w_proc_h, processed, own, mixes, tops, mesh_both, att_both, w_out, w_near, w_proc, mixed, sems):
    rows, width = mixed.shape
    pairs = width // LANES
    upper, lower = pl.ds(0, rows), pl.ds(rows, rows)
    copies = fetch(
        [
            (att_prev_h, att_both.at[upper]),
            (att_next_h, att_both.at[lower]),
            (w_out_h, w_out),
            (mesh_prev_h, mesh_both.at[upper]),
            (mesh_next_h, mesh_both.at[lower]),
            (w_qkv_h.at[:, pl.ds(width, 2 * width)], w_near),
            (own_h, own),
            (mixes_h, mixes),
            (tops_h, tops),
            (w_proc_h, w_proc),
        ],
        sems,
    )
    for item in copies[:5]:
        item.wait()
    near = (mesh_both[...].astype(jnp.float32) + mm(att_both[...], w_out[...])).astype(jnp.bfloat16)
    normed = norm_rows(near)
    copies[5].wait()
    near_kv = mm(normed, w_near[...]).astype(jnp.bfloat16)
    for item in copies[6:]:
        item.wait()
    behind = lax.broadcasted_iota(jnp.int32, (rows, rows), 1) >= lax.broadcasted_iota(jnp.int32, (rows, rows), 0)
    behind_f = behind.astype(jnp.float32)
    bias = behind_f * jnp.where(edges[0] > 0, 0.0, NEG) + (1.0 - behind_f) * jnp.where(edges[1] > 0, 0.0, NEG)
    low_half = lane_group((rows, LANES), LANES // 2) == 0
    masks = half_masks()
    scores, softs, sums = {}, {}, {}
    for turn in range(HEADS + 2):
        if turn < HEADS:
            lanes = slice(turn // 2 * LANES, (turn // 2 + 1) * LANES)
            both = mm_nt(own[:, lanes], near_kv[:, lanes] * masks[turn % 2])
            scores[turn] = jnp.where(behind, both[:, :rows], both[:, rows:]) + bias
        head = turn - 1
        if 0 <= head < HEADS:
            item = scores.pop(head)
            top = jnp.max(item, axis=-1, keepdims=True)
            term = jnp.exp2(item - top)
            first = jnp.where(behind, term, 0.0)
            softs[head] = (top, jnp.concatenate([first, term - first], axis=1).astype(jnp.bfloat16))
        head = turn - 2
        if head < 0:
            continue
        pair, half = divmod(head, 2)
        value = near_kv[:, width + pair * LANES:width + (pair + 1) * LANES]
        table = jnp.concatenate([value * masks[half], jnp.broadcast_to(masks[half], value.shape)], axis=1)
        sums[half] = mm(softs[head][1], table)
        if half:
            top = jnp.where(low_half, softs.pop(head - 1)[0], softs.pop(head)[0])
            best = jnp.maximum(top, tops[pair])
            near_part, own_part = jnp.exp2(top - best), jnp.exp2(tops[pair] - best)
            total = sums[0] + sums[1]
            share = total[:, :LANES] * near_part + mixes[pair, :, :LANES] * own_part
            count = total[:, LANES:] * near_part + mixes[pair, :, LANES:] * own_part
            mixed[:, pair * LANES:(pair + 1) * LANES] = (share / count).astype(jnp.bfloat16)
    processed[...] = (own[:, width:].astype(jnp.float32) + mm(mixed[...], w_proc[...])).astype(jnp.bfloat16)


def call(kernel, name, outs, out_specs, operands, scratch, cost, limit=LIMIT):
    return pl.pallas_call(
        kernel,
        name=name,
        out_shape=outs,
        in_specs=[SMEM if item.shape == (2,) else ANY for item in operands],
        out_specs=out_specs,
        scratch_shapes=scratch,
        cost_estimate=pl.CostEstimate(flops=cost[0], bytes_accessed=cost[1], transcendentals=cost[2]),
        compiler_params=pltpu.CompilerParams(vmem_limit_bytes=limit),
    )(*operands)


def shape(dims, dtype=jnp.bfloat16):
    return jax.ShapeDtypeStruct(dims, dtype)


def held(item):
    return pltpu.VMEM(item.shape, item.dtype)


def dma(count):
    return pltpu.SemaphoreType.DMA((count,))


def local(grid_feats, mesh_feats, routes, edge_first, edge_count, w_query, w_kv, w_out_enc, w_qkv, w_out_proc):
    width = w_query.shape[1]
    model = mesh_feats.shape[1]
    query_scale = math.log2(math.e) / math.sqrt(width // HEADS)
    node_count = lax.axis_size("outer") * lax.axis_size("inner")
    block_count, route_count = routes.shape
    rows = mesh_feats.shape[0]
    key_count = grid_feats.shape[0]
    block_len = rows // block_count
    capacity = max(1, (block_count * route_count + node_count - 1) // node_count)
    pairs = width // LANES
    pair_rows = capacity * block_len
    note_rows = max(8, -(-2 * capacity // 8) * 8)
    message = shape((node_count, pairs * pair_rows + note_rows, LANES))
    message_bytes = 2 * math.prod(message.shape)
    routes_t, first_t, count_t = routes.T, edge_first.T, edge_count.T
    ranks_shape = shape(routes_t.shape, jnp.int32)
    in_smem = pltpu.SMEM(routes_t.shape, jnp.int32)
    place = (block_len, capacity)

    send, ranks = call(
        functools.partial(send_kernel, *place, query_scale),
        "send_queries",
        [message, ranks_shape],
        [VMEM, SMEM],
        (routes_t, first_t, count_t, mesh_feats, w_query),
        [in_smem, held(first_t), held(count_t), held(mesh_feats), held(w_query), pltpu.SMEM((node_count,), jnp.int32),
         pltpu.VMEM((node_count * note_rows, LANES), jnp.float32), dma(5)],
        (2 * rows * model * width, 2 * model * (rows + width) + message_bytes, 0),
        None,
    )
    recv = lax.all_to_all(send, AXES, split_axis=0, concat_axis=0, tiled=True)

    table = call(
        grid_kernel,
        "grid_keys",
        shape((pairs, 3 * key_count, 2 * LANES)),
        VMEM,
        (grid_feats, w_kv),
        [held(grid_feats), held(w_kv), dma(2)],
        (4 * key_count * model * width, 2 * model * (key_count + 2 * width) + 12 * key_count * width, 0),
        None,
    )

    forward = [(i, i + 1) for i in range(node_count - 1)]
    backward = [(i + 1, i) for i in range(node_count - 1)]
    late_mesh, table = lax.optimization_barrier((mesh_feats, table))
    mesh_prev = lax.ppermute(late_mesh, AXES, forward)
    mesh_next = lax.ppermute(late_mesh, AXES, backward)

    chunk = math.gcd(node_count * pair_rows, 512)
    back = call(
        functools.partial(owner_kernel, *place, chunk),
        "owner_attention",
        message,
        HBM,
        (recv, table),
        [held(message), held(table), held(message),
         pltpu.VMEM((node_count * pair_rows, key_count), jnp.float32), dma(2), dma(node_count * pair_rows // chunk)],
        (4 * node_count * pair_rows * key_count * width, 2 * message_bytes, node_count * pair_rows * key_count * HEADS),
    )
    back = lax.all_to_all(back, AXES, split_axis=0, concat_axis=0, tiled=True)

    attended = call(
        functools.partial(combine_kernel, *place),
        "combine_routes",
        shape((rows, width)),
        VMEM,
        (routes_t, ranks, back),
        [in_smem, in_smem, held(message), pltpu.VMEM((node_count * HEADS, LANES), jnp.float32), dma(4)],
        (4 * rows * width * route_count, message_bytes, 0),
    )
    att_prev = lax.ppermute(attended, AXES, forward)
    att_next = lax.ppermute(attended, AXES, backward)

    encoded, own, mixes, tops = call(
        functools.partial(own_kernel, query_scale),
        "own_rows",
        [shape((rows, model)), shape((rows, width + model)), shape((pairs, rows, 2 * LANES), jnp.float32),
         shape((pairs, rows, LANES), jnp.float32)],
        [VMEM] * 4,
        (mesh_feats, attended, w_out_enc, w_qkv),
        [held(mesh_feats), held(attended), held(w_out_enc), held(w_qkv), dma(4)],
        (8 * rows * model * width, 2 * model * (2 * rows + 4 * width), 0),
    )

    place_index = lax.axis_index(AXES)
    edges = jnp.stack([place_index > 0, place_index < node_count - 1]).astype(jnp.int32)
    processed = call(
        window_kernel,
        "window_attention",
        shape((rows, model)),
        VMEM,
        (edges, own, mixes, tops, mesh_prev, mesh_next, att_prev, att_next, w_out_enc, w_qkv, w_out_proc),
        [held(own), held(mixes), held(tops), pltpu.VMEM((2 * rows, model), jnp.bfloat16),
         pltpu.VMEM((2 * rows, width), jnp.bfloat16), held(w_out_enc), pltpu.VMEM((model, 2 * width), jnp.bfloat16),
         held(w_out_proc), pltpu.VMEM((rows, width), jnp.bfloat16), dma(10)],
        (16 * rows * model * width, 2 * model * (4 * rows + 5 * width), 3 * rows * rows * HEADS),
    )
    return (encoded, processed)


def solution(mesh):
    rows = P(("groups", "outer", "inner"), None)
    return jax.shard_map(
        local,
        mesh=mesh,
        in_specs=(rows,) * 5 + (P(),) * 5,
        out_specs=(rows, rows),
        check_vma=False,
    )
```

```python
import functools
import math

import jax
import jax.numpy as jnp
from jax import lax
from jax.experimental import pallas as pl
from jax.experimental.pallas import tpu as pltpu
from jax.sharding import PartitionSpec as P

HEADS = 8
WIN = 512
LANES = 128
NEG = -1e30
AXES = ("outer", "inner")
VMEM = pl.BlockSpec(memory_space=pltpu.VMEM)
SMEM = pl.BlockSpec(memory_space=pltpu.SMEM)
ANY = pl.BlockSpec(memory_space=pl.ANY)
HBM = pl.BlockSpec(memory_space=pltpu.HBM)
LIMIT = 50 << 20


def norm_rows(inputs):
    as_float = inputs.astype(jnp.float32)
    row_mean = jnp.mean(as_float, axis=-1, keepdims=True)
    centered = as_float - row_mean
    variance = jnp.mean(centered * centered, axis=-1, keepdims=True)
    return (centered * lax.rsqrt(variance + 1e-05)).astype(jnp.bfloat16)


def mm(a, b):
    return jnp.dot(a, b, preferred_element_type=jnp.float32)


def mm_nt(a, b):
    return lax.dot_general(a, b, (((1,), (1,)), ((), ())), preferred_element_type=jnp.float32)


def mm_tn(a, b):
    return lax.dot_general(a, b, (((0,), (0,)), ((), ())), preferred_element_type=jnp.float32)


def lane_group(shape, width):
    return lax.broadcasted_iota(jnp.int32, shape, len(shape) - 1) // width


def half_masks():
    low = (lane_group((1, LANES), LANES // 2) == 0).astype(jnp.float32)
    return low.astype(jnp.bfloat16), (1.0 - low).astype(jnp.bfloat16)


def fetch(pairs, sems):
    copies = [pltpu.make_async_copy(src, dst, sems.at[i]) for i, (src, dst) in enumerate(pairs)]
    for item in copies:
        item.start()
    return copies


def send_kernel(block_len, capacity, query_scale, spot_h, routes_h, first_h, count_h, mesh_h, w_query_h, *refs):
    send_h, ranks, *near_h, mine, routes, first, count, mesh, w_query, send, tally, notes, sems, outs = refs
    copies = fetch(
        [
            (mesh_h, mesh),
            (w_query_h, w_query),
            (routes_h, routes),
            (first_h, first),
            (count_h, count),
            (spot_h, mine),
        ],
        sems,
    )
    route_count, block_count = routes.shape
    node_count = send.shape[0]
    pair_rows = capacity * block_len
    pairs = w_query.shape[1] // LANES
    note_rows = send.shape[1] - pairs * pair_rows

    def clear(i, carry):
        tally[i] = 0
        return carry

    lax.fori_loop(0, node_count, clear, 0)
    if node_count * capacity != block_count * route_count:
        send[...] = jnp.zeros(send.shape, send.dtype)
    notes[...] = jnp.zeros(notes.shape, notes.dtype)
    copies[0].wait()
    normed = norm_rows(mesh[...])
    for item in copies[1:]:
        item.wait()
    first_all = first[...]
    upper = first_all >= 256
    low_part = jnp.where(upper, first_all - 256, first_all).astype(jnp.float32)
    signed = jnp.where(upper, -count[...], count[...]).astype(jnp.float32)
    group = lane_group((1, LANES), block_len)
    per_tile = LANES // block_len
    queries = (mm(normed, w_query[...]) * query_scale).astype(jnp.bfloat16)
    for block in range(block_count):
        tile, spot = divmod(block, per_tile)
        cols = slice(tile * LANES, (tile + 1) * LANES)
        rows = slice(block * block_len, (block + 1) * block_len)
        for route in range(route_count):
            owner = routes[route, block]
            rank = tally[owner]
            tally[owner] = rank + 1
            ranks[route, block] = rank
            for pair in range(pairs):
                start = pl.multiple_of(pair * pair_rows + rank * block_len, block_len)
                send[owner, pl.ds(start, block_len), :] = queries[rows, pair * LANES:(pair + 1) * LANES]
            note = owner * note_rows + 2 * rank
            keep = group == spot
            notes[pl.ds(note, 1), :] = jnp.where(keep, low_part[route:route + 1, cols], 0.0)
            notes[pl.ds(note + 1, 1), :] = jnp.where(keep, signed[route:route + 1, cols], 0.0)
    for owner in range(node_count):
        send[owner, pairs * pair_rows:, :] = notes[owner * note_rows:(owner + 1) * note_rows, :].astype(jnp.bfloat16)
    moves = [(send, send_h)]
    for turn, item in enumerate(near_h):
        moves.append((send.at[mine[0] ^ (turn + 1)], item))
    for item in fetch(moves, outs):
        item.wait()


def grid_kernel(grid_h, w_kv_h, table, grid, w_kv, sems):
    copies = fetch([(grid_h, grid), (w_kv_h, w_kv)], sems)
    width = w_kv.shape[1] // 2
    copies[0].wait()
    normed = norm_rows(grid[...])
    copies[1].wait()
    grid_kv = mm(normed, w_kv[...]).astype(jnp.bfloat16)
    count = grid_kv.shape[0]
    masks = half_masks()
    for pair in range(width // LANES):
        key_pair = grid_kv[:, pair * LANES:(pair + 1) * LANES]
        value_pair = grid_kv[:, width + pair * LANES:width + (pair + 1) * LANES]
        for half in range(2):
            mask = masks[half]
            rows = slice(half * count, (half + 1) * count)
            table[pair, rows, :LANES] = value_pair * mask
            table[pair, rows, LANES:] = jnp.broadcast_to(mask, (count, LANES))
            table[pair, 2 * count:, half * LANES:(half + 1) * LANES] = key_pair * mask


def attend(block_len, capacity, chunk, recv, table, back, bias, ready, finished):
    node_count, message_rows, _ = recv.shape
    pairs, table_rows, _ = table.shape
    key_count = table_rows // 3
    pair_rows = capacity * block_len
    note_rows = message_rows - pairs * pair_rows
    row_count = node_count * pair_rows
    group = chunk // pair_rows
    chunks = row_count // chunk
    tags = recv[:, pairs * pair_rows:, :].reshape(node_count * note_rows, LANES)
    fold = (
        lax.broadcasted_iota(jnp.int32, (block_len, LANES), 1) % block_len
        == lax.broadcasted_iota(jnp.int32, (block_len, LANES), 0)
    ).astype(jnp.float32).astype(jnp.bfloat16)
    columns = mm_nt(fold, tags)
    key_pos = lax.broadcasted_iota(jnp.int32, (block_len, key_count), 1).astype(jnp.float32)
    for owner in range(node_count):
        for rank in range(capacity):
            spot = owner * note_rows + 2 * rank
            low_part, signed = columns[:, spot:spot + 1], columns[:, spot + 1:spot + 2]
            begin = low_part + jnp.where(signed < 0, 256.0, 0.0)
            end = begin + jnp.maximum(jnp.abs(signed), 1.0)
            inside = (key_pos >= begin) & (key_pos < end)
            row = (owner * capacity + rank) * block_len
            bias[row:row + block_len, :] = jnp.where(inside, 0.0, NEG)
    ready()
    low_half = lane_group((chunk, LANES), LANES // 2) == 0
    pick_row = lax.broadcasted_iota(jnp.int32, (HEADS, LANES), 0)
    pick_lane = lax.broadcasted_iota(jnp.int32, (HEADS, LANES), 1)
    half_lane = lane_group((HEADS, LANES), LANES // 2)

    def step(index, carry):
        span = pl.ds(index * group, group)
        mask = bias[pl.ds(pl.multiple_of(index * chunk, chunk), chunk), :]
        log_high = jnp.zeros((HEADS, chunk), jnp.float32)
        log_low = jnp.zeros((HEADS, chunk), jnp.float32)
        scores, softs, mixes = {}, {}, {}
        for turn in range(HEADS + 4):
            if turn < HEADS:
                pair = turn // 2
                rows = recv[span, pair * pair_rows:(pair + 1) * pair_rows, :].reshape(chunk, LANES)
                half = turn % 2
                scores[turn] = mm_nt(rows, table[pair, 2 * key_count:, half * LANES:(half + 1) * LANES]) + mask
            head = turn - 2
            if 0 <= head < HEADS:
                item = scores.pop(head)
                top = jnp.max(item, axis=-1, keepdims=True)
                softs[head] = (top, jnp.exp2(item - top).astype(jnp.bfloat16))
            head = turn - 4
            if head < 0:
                continue
            pair, half = divmod(head, 2)
            mixes[head] = mm(softs[head][1], table[pair, half * key_count:(half + 1) * key_count, :])
            if half == 0:
                continue
            mixed = mixes.pop(head - 1) + mixes.pop(head)
            total = mixed[:, LANES:]
            part = slice(pair * pair_rows, (pair + 1) * pair_rows)
            back[span, part, :] = (mixed[:, :LANES] / total).astype(jnp.bfloat16).reshape(group, pair_rows, LANES)
            logs = jnp.where(low_half, softs.pop(head - 1)[0], softs.pop(head)[0]) + jnp.log2(total)
            high = logs.astype(jnp.bfloat16)
            low = (logs - high.astype(jnp.float32)).astype(jnp.bfloat16)
            pick = (
                ((pick_row == 2 * pair) & (pick_lane == 0)) | ((pick_row == 2 * pair + 1) & (pick_lane == LANES // 2))
            ).astype(jnp.float32).astype(jnp.bfloat16)
            log_high = log_high + mm_nt(pick, high)
            log_low = log_low + mm_nt(pick, low)
        for offset in range(group):
            lane = offset * pair_rows
            tile, shift = lane // LANES, lane % LANES
            high = log_high[:, tile * LANES:(tile + 1) * LANES]
            low = log_low[:, tile * LANES:(tile + 1) * LANES]
            if shift:
                high = pltpu.roll(high, LANES - shift, 1)
            low_shift = (LANES // 2 - shift) % LANES
            if low_shift:
                low = pltpu.roll(low, low_shift, 1)
            back[index * group + offset, pairs * pair_rows:pairs * pair_rows + HEADS, :] = jnp.where(
                half_lane == 0, high, low
            ).astype(jnp.bfloat16)
        finished(index, span)
        return carry

    lax.fori_loop(0, chunks, step, 0)


def all_kernel(block_len, capacity, chunk, recv_h, table_h, back_h, recv, table, back, bias, sems, outs):
    copies = fetch([(recv_h, recv), (table_h, table)], sems)
    copies[0].wait()

    def finished(index, span):
        pltpu.make_async_copy(back.at[span], back_h.at[span], outs.at[index]).start()

    attend(block_len, capacity, chunk, recv, table, back, bias, copies[1].wait, finished)
    group = chunk // (capacity * block_len)
    for index in range(recv.shape[0] // group):
        span = pl.ds(index * group, group)
        pltpu.make_async_copy(back.at[span], back_h.at[span], outs.at[index]).wait()


def near_kernel(block_len, capacity, chunk, spot_h, send_h, *refs):
    count = len(refs) - 9
    near_h, (table_h, back_h, spot, recv, table, back, bias, sems, outs) = refs[:count], refs[count:]
    first = pltpu.make_async_copy(spot_h, spot, sems.at[0])
    first.start()
    copies = [pltpu.make_async_copy(table_h, table, sems.at[1])]
    for turn, item in enumerate(near_h):
        copies.append(pltpu.make_async_copy(item, recv.at[turn + 1], sems.at[turn + 3]))
    for item in copies:
        item.start()
    first.wait()
    own = pltpu.make_async_copy(send_h.at[spot[0]], recv.at[0], sems.at[2])
    own.start()
    own.wait()
    for item in copies[1:]:
        item.wait()
    attend(block_len, capacity, chunk, recv, table, back, bias, copies[0].wait, lambda index, span: None)
    last = pltpu.make_async_copy(back, back_h, outs)
    last.start()
    last.wait()


def far_kernel(block_len, capacity, chunk, spot_h, recv_h, near_h, table_h, back_h, spot, recv, near, table, back, bias,
               sems, outs):
    half = recv.shape[0]
    copies = fetch([(spot_h, spot), (near_h, near), (table_h, table)], sems)
    copies[0].wait()
    base = half - spot[0] // half * half
    load = pltpu.make_async_copy(recv_h.at[pl.ds(base, half)], recv, sems.at[3])
    load.start()
    copies[1].wait()
    moves = fetch([(near.at[turn], back_h.at[spot[0] ^ turn]) for turn in range(half)], outs)
    load.wait()
    group = chunk // (capacity * block_len)

    def result(index, span):
        return pltpu.make_async_copy(back.at[span], back_h.at[pl.ds(base + index * group, group)], outs.at[half + index])

    attend(block_len, capacity, chunk, recv, table, back, bias, copies[2].wait, lambda index, span: result(index, span).start())
    for item in moves:
        item.wait()
    for index in range(half // group):
        result(index, pl.ds(index * group, group)).wait()


def combine_kernel(block_len, capacity, routes_h, ranks_h, back_h, attended, routes, ranks, back, logs, sems):
    node_count, message_rows, _ = back.shape
    width = attended.shape[1]
    pairs = width // LANES
    pair_rows = capacity * block_len
    copies = fetch(
        [
            (routes_h, routes),
            (ranks_h, ranks),
            (back_h.at[:, pl.ds(pairs * pair_rows, HEADS)], back.at[:, pl.ds(pairs * pair_rows, HEADS)]),
            (back_h.at[:, pl.ds(0, pairs * pair_rows)], back.at[:, pl.ds(0, pairs * pair_rows)]),
        ],
        sems,
    )
    route_count, block_count = routes.shape
    for item in copies[:3]:
        item.wait()
    halves = back[:, pairs * pair_rows:pairs * pair_rows + HEADS, :].astype(jnp.float32).reshape(node_count * HEADS, LANES)
    logs[...] = halves + pltpu.roll(halves, LANES // 2, 1)
    group = lane_group((HEADS, LANES), block_len)
    per_tile = LANES // block_len
    tiles = block_count // per_tile
    route_logs = []
    for route in range(route_count):
        parts = []
        for tile in range(tiles):
            gathered = jnp.zeros((HEADS, LANES), jnp.float32)
            for spot in range(per_tile):
                block = tile * per_tile + spot
                start = pl.multiple_of(routes[route, block] * HEADS, HEADS)
                shift = (spot + per_tile - ranks[route, block]) * block_len % LANES
                moved = pltpu.roll(logs[pl.ds(start, HEADS), :], shift, 1)
                gathered = jnp.where(group == spot, moved, gathered)
            parts.append(gathered)
        route_logs.append(jnp.concatenate(parts, axis=1))
    best = functools.reduce(jnp.maximum, route_logs)
    terms = [jnp.exp2(item - best) for item in route_logs]
    total = functools.reduce(jnp.add, terms)
    spread = (
        lax.broadcasted_iota(jnp.int32, (2 * HEADS, width), 1) // (width // HEADS)
        == lax.broadcasted_iota(jnp.int32, (2 * HEADS, width), 0) % HEADS
    ).astype(jnp.float32).astype(jnp.bfloat16)
    weights = []
    for item in terms:
        share = item / total
        high = share.astype(jnp.bfloat16).astype(jnp.float32)
        both = jnp.concatenate([high, share - high], axis=0).astype(jnp.bfloat16)
        weights.append(mm_tn(both, spread))
    copies[3].wait()
    for block in range(block_count):
        rows = slice(block * block_len, (block + 1) * block_len)
        for pair in range(pairs):
            lanes = slice(pair * LANES, (pair + 1) * LANES)
            acc = None
            for route in range(route_count):
                start = pl.multiple_of(pair * pair_rows + ranks[route, block] * block_len, block_len)
                piece = back[routes[route, block], pl.ds(start, block_len), :].astype(jnp.float32)
                piece = piece * weights[route][rows, lanes]
                acc = piece if acc is None else acc + piece
            attended[rows, lanes] = acc.astype(jnp.bfloat16)


def own_kernel(query_scale, mesh_h, attended_h, w_out_h, w_qkv_h, encoded, own, mixes, tops,
               mesh, attended, w_out, w_qkv, sems):
    copies = fetch([(attended_h, attended), (w_out_h, w_out), (mesh_h, mesh), (w_qkv_h, w_qkv)], sems)
    width = attended.shape[1]
    for item in copies[:3]:
        item.wait()
    rows = (mesh[...].astype(jnp.float32) + mm(attended[...], w_out[...])).astype(jnp.bfloat16)
    encoded[...] = rows
    own[:, width:] = rows
    normed = norm_rows(rows)
    copies[3].wait()
    query = (mm(normed, w_qkv[:, :width]) * query_scale).astype(jnp.bfloat16)
    own[:, :width] = query
    keyval = mm(normed, w_qkv[:, width:]).astype(jnp.bfloat16)
    low_half = lane_group((rows.shape[0], LANES), LANES // 2) == 0
    masks = half_masks()
    scores, softs, mixed = {}, {}, {}
    for turn in range(HEADS + 2):
        if turn < HEADS:
            lanes = slice(turn // 2 * LANES, (turn // 2 + 1) * LANES)
            scores[turn] = mm_nt(query[:, lanes], keyval[:, lanes] * masks[turn % 2])
        head = turn - 1
        if 0 <= head < HEADS:
            item = scores.pop(head)
            top = jnp.max(item, axis=-1, keepdims=True)
            softs[head] = (top, jnp.exp2(item - top).astype(jnp.bfloat16))
        head = turn - 2
        if head < 0:
            continue
        pair, half = divmod(head, 2)
        value = keyval[:, width + pair * LANES:width + (pair + 1) * LANES]
        table = jnp.concatenate([value * masks[half], jnp.broadcast_to(masks[half], value.shape)], axis=1)
        mixed[half] = mm(softs[head][1], table)
        if half:
            mixes[pair] = mixed[0] + mixed[1]
            tops[pair] = jnp.where(low_half, softs.pop(head - 1)[0], softs.pop(head)[0])


def window_kernel(edges, own_h, mixes_h, tops_h, mesh_prev_h, mesh_next_h, att_prev_h, att_next_h, w_out_h, w_qkv_h,
                  w_proc_h, processed, own, mixes, tops, mesh_both, att_both, w_out, w_near, w_proc, mixed, sems):
    rows, width = mixed.shape
    pairs = width // LANES
    upper, lower = pl.ds(0, rows), pl.ds(rows, rows)
    copies = fetch(
        [
            (att_prev_h, att_both.at[upper]),
            (att_next_h, att_both.at[lower]),
            (w_out_h, w_out),
            (mesh_prev_h, mesh_both.at[upper]),
            (mesh_next_h, mesh_both.at[lower]),
            (w_qkv_h.at[:, pl.ds(width, 2 * width)], w_near),
            (own_h, own),
            (mixes_h, mixes),
            (tops_h, tops),
            (w_proc_h, w_proc),
        ],
        sems,
    )
    for item in copies[:5]:
        item.wait()
    near = (mesh_both[...].astype(jnp.float32) + mm(att_both[...], w_out[...])).astype(jnp.bfloat16)
    normed = norm_rows(near)
    copies[5].wait()
    near_kv = mm(normed, w_near[...]).astype(jnp.bfloat16)
    for item in copies[6:]:
        item.wait()
    behind = lax.broadcasted_iota(jnp.int32, (rows, rows), 1) >= lax.broadcasted_iota(jnp.int32, (rows, rows), 0)
    behind_f = behind.astype(jnp.float32)
    bias = behind_f * jnp.where(edges[0] > 0, 0.0, NEG) + (1.0 - behind_f) * jnp.where(edges[1] > 0, 0.0, NEG)
    low_half = lane_group((rows, LANES), LANES // 2) == 0
    masks = half_masks()
    scores, softs, sums = {}, {}, {}
    for turn in range(HEADS + 2):
        if turn < HEADS:
            lanes = slice(turn // 2 * LANES, (turn // 2 + 1) * LANES)
            both = mm_nt(own[:, lanes], near_kv[:, lanes] * masks[turn % 2])
            scores[turn] = jnp.where(behind, both[:, :rows], both[:, rows:]) + bias
        head = turn - 1
        if 0 <= head < HEADS:
            item = scores.pop(head)
            top = jnp.max(item, axis=-1, keepdims=True)
            term = jnp.exp2(item - top)
            first = jnp.where(behind, term, 0.0)
            softs[head] = (top, jnp.concatenate([first, term - first], axis=1).astype(jnp.bfloat16))
        head = turn - 2
        if head < 0:
            continue
        pair, half = divmod(head, 2)
        value = near_kv[:, width + pair * LANES:width + (pair + 1) * LANES]
        table = jnp.concatenate([value * masks[half], jnp.broadcast_to(masks[half], value.shape)], axis=1)
        sums[half] = mm(softs[head][1], table)
        if half:
            top = jnp.where(low_half, softs.pop(head - 1)[0], softs.pop(head)[0])
            best = jnp.maximum(top, tops[pair])
            near_part, own_part = jnp.exp2(top - best), jnp.exp2(tops[pair] - best)
            total = sums[0] + sums[1]
            share = total[:, :LANES] * near_part + mixes[pair, :, :LANES] * own_part
            count = total[:, LANES:] * near_part + mixes[pair, :, LANES:] * own_part
            mixed[:, pair * LANES:(pair + 1) * LANES] = (share / count).astype(jnp.bfloat16)
    processed[...] = (own[:, width:].astype(jnp.float32) + mm(mixed[...], w_proc[...])).astype(jnp.bfloat16)


def call(kernel, name, outs, out_specs, operands, scratch, cost, limit=LIMIT):
    return pl.pallas_call(
        kernel,
        name=name,
        out_shape=outs,
        in_specs=[SMEM if item.shape == (2,) else ANY for item in operands],
        out_specs=out_specs,
        scratch_shapes=scratch,
        cost_estimate=pl.CostEstimate(flops=cost[0], bytes_accessed=cost[1], transcendentals=cost[2]),
        compiler_params=pltpu.CompilerParams(vmem_limit_bytes=limit),
    )(*operands)


def shape(dims, dtype=jnp.bfloat16):
    return jax.ShapeDtypeStruct(dims, dtype)


def held(item):
    return pltpu.VMEM(item.shape, item.dtype)


def dma(count):
    return pltpu.SemaphoreType.DMA((count,))


def local(grid_feats, mesh_feats, routes, edge_first, edge_count, w_query, w_kv, w_out_enc, w_qkv, w_out_proc):
    width = w_query.shape[1]
    model = mesh_feats.shape[1]
    query_scale = math.log2(math.e) / math.sqrt(width // HEADS)
    node_count = lax.axis_size("outer") * lax.axis_size("inner")
    block_count, route_count = routes.shape
    rows = mesh_feats.shape[0]
    key_count = grid_feats.shape[0]
    block_len = rows // block_count
    capacity = max(1, (block_count * route_count + node_count - 1) // node_count)
    pairs = width // LANES
    pair_rows = capacity * block_len
    note_rows = max(8, -(-2 * capacity // 8) * 8)
    message = shape((node_count, pairs * pair_rows + note_rows, LANES))
    message_bytes = 2 * math.prod(message.shape)
    routes_t, first_t, count_t = routes.T, edge_first.T, edge_count.T
    ranks_shape = shape(routes_t.shape, jnp.int32)
    in_smem = pltpu.SMEM(routes_t.shape, jnp.int32)
    place = (block_len, capacity)

    place_index = lax.axis_index(AXES)
    spot = place_index.reshape(1).astype(jnp.int32)
    half = node_count // 2
    split = node_count == 16
    near_count = half - 1 if split else 0
    one = shape(message.shape[1:])
    spot_smem = pltpu.SMEM((1,), jnp.int32)

    send, ranks, *near = call(
        functools.partial(send_kernel, *place, query_scale),
        "send_queries",
        [message, ranks_shape] + [one] * near_count,
        [ANY, SMEM] + [ANY] * near_count,
        (spot, routes_t, first_t, count_t, mesh_feats, w_query),
        [spot_smem, in_smem, held(first_t), held(count_t), held(mesh_feats), held(w_query), held(message),
         pltpu.SMEM((node_count,), jnp.int32), pltpu.VMEM((node_count * note_rows, LANES), jnp.float32), dma(6),
         dma(1 + near_count)],
        (2 * rows * model * width, 2 * model * (rows + width) + message_bytes, 0),
        None,
    )
    recv = lax.all_to_all(send, AXES, split_axis=0, concat_axis=0, tiled=True)

    table = call(
        grid_kernel,
        "grid_keys",
        shape((pairs, 3 * key_count, 2 * LANES)),
        VMEM,
        (grid_feats, w_kv),
        [held(grid_feats), held(w_kv), dma(2)],
        (4 * key_count * model * width, 2 * model * (key_count + 2 * width) + 12 * key_count * width, 0),
        None,
    )

    forward = [(i, i + 1) for i in range(node_count - 1)]
    backward = [(i + 1, i) for i in range(node_count - 1)]

    def attend_cost(count):
        work = count * pair_rows * key_count
        return 4 * work * width, 2 * message_bytes, work * HEADS

    def attend_scratch(count):
        part = shape((count,) + message.shape[1:])
        return [held(part), held(table), held(part), pltpu.VMEM((count * pair_rows, key_count), jnp.float32)]

    if split:
        *near, table = lax.optimization_barrier((*near, table))
        near = [
            lax.ppermute(item, AXES, [(i, i ^ (turn + 1)) for i in range(node_count)]) for turn, item in enumerate(near)
        ]
        chunk = math.gcd(half * pair_rows, 512)
        near_back = call(
            functools.partial(near_kernel, *place, chunk),
            "near_attention",
            shape((half,) + message.shape[1:]),
            HBM,
            (spot, send, *near, table),
            [spot_smem] + attend_scratch(half) + [dma(2 + half), pltpu.SemaphoreType.DMA],
            attend_cost(half),
        )
        late_mesh, near_back = lax.optimization_barrier((mesh_feats, near_back))
        recv_part, held_table, back_part, bias_part = attend_scratch(half)
        back = call(
            functools.partial(far_kernel, *place, chunk),
            "far_attention",
            message,
            HBM,
            (spot, recv, near_back, table),
            [spot_smem, recv_part, held(near_back), held_table, back_part, bias_part, dma(4),
             dma(half + half * pair_rows // chunk)],
            attend_cost(half),
        )
    else:
        late_mesh, table = lax.optimization_barrier((mesh_feats, table))
        chunk = math.gcd(node_count * pair_rows, 512)
        back = call(
            functools.partial(all_kernel, *place, chunk),
            "owner_attention",
            message,
            HBM,
            (recv, table),
            attend_scratch(node_count) + [dma(2), dma(node_count * pair_rows // chunk)],
            attend_cost(node_count),
        )
    mesh_prev = lax.ppermute(late_mesh, AXES, forward)
    mesh_next = lax.ppermute(late_mesh, AXES, backward)
    back = lax.all_to_all(back, AXES, split_axis=0, concat_axis=0, tiled=True)

    attended = call(
        functools.partial(combine_kernel, *place),
        "combine_routes",
        shape((rows, width)),
        VMEM,
        (routes_t, ranks, back),
        [in_smem, in_smem, held(message), pltpu.VMEM((node_count * HEADS, LANES), jnp.float32), dma(4)],
        (4 * rows * width * route_count, message_bytes, 0),
    )
    att_prev = lax.ppermute(attended, AXES, forward)
    att_next = lax.ppermute(attended, AXES, backward)

    encoded, own, mixes, tops = call(
        functools.partial(own_kernel, query_scale),
        "own_rows",
        [shape((rows, model)), shape((rows, width + model)), shape((pairs, rows, 2 * LANES), jnp.float32),
         shape((pairs, rows, LANES), jnp.float32)],
        [VMEM] * 4,
        (mesh_feats, attended, w_out_enc, w_qkv),
        [held(mesh_feats), held(attended), held(w_out_enc), held(w_qkv), dma(4)],
        (8 * rows * model * width, 2 * model * (2 * rows + 4 * width), 0),
    )

    edges = jnp.stack([place_index > 0, place_index < node_count - 1]).astype(jnp.int32)
    processed = call(
        window_kernel,
        "window_attention",
        shape((rows, model)),
        VMEM,
        (edges, own, mixes, tops, mesh_prev, mesh_next, att_prev, att_next, w_out_enc, w_qkv, w_out_proc),
        [held(own), held(mixes), held(tops), pltpu.VMEM((2 * rows, model), jnp.bfloat16),
         pltpu.VMEM((2 * rows, width), jnp.bfloat16), held(w_out_enc), pltpu.VMEM((model, 2 * width), jnp.bfloat16),
         held(w_out_proc), pltpu.VMEM((rows, width), jnp.bfloat16), dma(10)],
        (16 * rows * model * width, 2 * model * (4 * rows + 5 * width), 3 * rows * rows * HEADS),
    )
    return (encoded, processed)


def solution(mesh):
    rows = P(("groups", "outer", "inner"), None)
    return jax.shard_map(
        local,
        mesh=mesh,
        in_specs=(rows,) * 5 + (P(),) * 5,
        out_specs=(rows, rows),
        check_vma=False,
    )
```

```python
import functools
import math

import jax
import jax.numpy as jnp
from jax import lax
from jax.experimental import pallas as pl
from jax.experimental.pallas import tpu as pltpu
from jax.sharding import PartitionSpec as P

HEADS = 8
WIN = 512
LANES = 128
NEG = -1e30
AXES = ("outer", "inner")
VMEM = pl.BlockSpec(memory_space=pltpu.VMEM)
SMEM = pl.BlockSpec(memory_space=pltpu.SMEM)
ANY = pl.BlockSpec(memory_space=pl.ANY)
HBM = pl.BlockSpec(memory_space=pltpu.HBM)
LIMIT = 50 << 20


def norm_rows(inputs):
    as_float = inputs.astype(jnp.float32)
    row_mean = jnp.mean(as_float, axis=-1, keepdims=True)
    centered = as_float - row_mean
    variance = jnp.mean(centered * centered, axis=-1, keepdims=True)
    return (centered * lax.rsqrt(variance + 1e-05)).astype(jnp.bfloat16)


def mm(a, b):
    return jnp.dot(a, b, preferred_element_type=jnp.float32)


def mm_nt(a, b):
    return lax.dot_general(a, b, (((1,), (1,)), ((), ())), preferred_element_type=jnp.float32)


def mm_tn(a, b):
    return lax.dot_general(a, b, (((0,), (0,)), ((), ())), preferred_element_type=jnp.float32)


def lane_group(shape, width):
    return lax.broadcasted_iota(jnp.int32, shape, len(shape) - 1) // width


def half_masks():
    low = (lane_group((1, LANES), LANES // 2) == 0).astype(jnp.float32)
    return low.astype(jnp.bfloat16), (1.0 - low).astype(jnp.bfloat16)


def fetch(pairs, sems):
    copies = [pltpu.make_async_copy(src, dst, sems.at[i]) for i, (src, dst) in enumerate(pairs)]
    for item in copies:
        item.start()
    return copies


def send_kernel(block_len, capacity, query_scale, routes_h, first_h, count_h, mesh_h, w_query_h, send, ranks,
                routes, first, count, mesh, w_query, tally, notes, sems):
    copies = fetch(
        [(mesh_h, mesh), (w_query_h, w_query), (routes_h, routes), (first_h, first), (count_h, count)], sems
    )
    route_count, block_count = routes.shape
    node_count = send.shape[0]
    pair_rows = capacity * block_len
    pairs = w_query.shape[1] // LANES
    note_rows = send.shape[1] - pairs * pair_rows

    def clear(i, carry):
        tally[i] = 0
        return carry

    lax.fori_loop(0, node_count, clear, 0)
    if node_count * capacity != block_count * route_count:
        send[...] = jnp.zeros(send.shape, send.dtype)
    notes[...] = jnp.zeros(notes.shape, notes.dtype)
    copies[0].wait()
    normed = norm_rows(mesh[...])
    for item in copies[1:]:
        item.wait()
    first_all = first[...]
    upper = first_all >= 256
    low_part = jnp.where(upper, first_all - 256, first_all).astype(jnp.float32)
    signed = jnp.where(upper, -count[...], count[...]).astype(jnp.float32)
    group = lane_group((1, LANES), block_len)
    per_tile = LANES // block_len
    queries = (mm(normed, w_query[...]) * query_scale).astype(jnp.bfloat16)
    for block in range(block_count):
        tile, spot = divmod(block, per_tile)
        cols = slice(tile * LANES, (tile + 1) * LANES)
        rows = slice(block * block_len, (block + 1) * block_len)
        for route in range(route_count):
            owner = routes[route, block]
            rank = tally[owner]
            tally[owner] = rank + 1
            ranks[route, block] = rank
            for pair in range(pairs):
                start = pl.multiple_of(pair * pair_rows + rank * block_len, block_len)
                send[owner, pl.ds(start, block_len), :] = queries[rows, pair * LANES:(pair + 1) * LANES]
            note = owner * note_rows + 2 * rank
            keep = group == spot
            notes[pl.ds(note, 1), :] = jnp.where(keep, low_part[route:route + 1, cols], 0.0)
            notes[pl.ds(note + 1, 1), :] = jnp.where(keep, signed[route:route + 1, cols], 0.0)
    for owner in range(node_count):
        send[owner, pairs * pair_rows:, :] = notes[owner * note_rows:(owner + 1) * note_rows, :].astype(jnp.bfloat16)


def grid_kernel(grid_h, w_kv_h, table, grid, w_kv, sems):
    copies = fetch([(grid_h, grid), (w_kv_h, w_kv)], sems)
    width = w_kv.shape[1] // 2
    copies[0].wait()
    normed = norm_rows(grid[...])
    copies[1].wait()
    grid_kv = mm(normed, w_kv[...]).astype(jnp.bfloat16)
    count = grid_kv.shape[0]
    masks = half_masks()
    for pair in range(width // LANES):
        key_pair = grid_kv[:, pair * LANES:(pair + 1) * LANES]
        value_pair = grid_kv[:, width + pair * LANES:width + (pair + 1) * LANES]
        for half in range(2):
            mask = masks[half]
            rows = slice(half * count, (half + 1) * count)
            table[pair, rows, :LANES] = value_pair * mask
            table[pair, rows, LANES:] = jnp.broadcast_to(mask, (count, LANES))
            table[pair, 2 * count:, half * LANES:(half + 1) * LANES] = key_pair * mask


def owner_kernel(block_len, capacity, chunk, recv, table_h, back_h, table, back, bias, sems, outs):
    node_count, message_rows, _ = recv.shape
    pairs, table_rows, _ = table.shape
    key_count = table_rows // 3
    pair_rows = capacity * block_len
    note_rows = message_rows - pairs * pair_rows
    group = chunk // pair_rows
    chunks = node_count // group
    copies = fetch([(table_h.at[pair], table.at[pair]) for pair in range(pairs)], sems)
    tags = recv[:, pairs * pair_rows:, :].reshape(node_count * note_rows, LANES)
    fold = (
        lax.broadcasted_iota(jnp.int32, (block_len, LANES), 1) % block_len
        == lax.broadcasted_iota(jnp.int32, (block_len, LANES), 0)
    ).astype(jnp.float32).astype(jnp.bfloat16)
    columns = mm_nt(fold, tags)
    key_pos = lax.broadcasted_iota(jnp.int32, (block_len, key_count), 1).astype(jnp.float32)

    def make_bias(index):
        for slot in range(index * group * capacity, (index + 1) * group * capacity):
            spot = slot // capacity * note_rows + 2 * (slot % capacity)
            low_part, signed = columns[:, spot:spot + 1], columns[:, spot + 1:spot + 2]
            begin = low_part + jnp.where(signed < 0, 256.0, 0.0)
            end = begin + jnp.maximum(jnp.abs(signed), 1.0)
            inside = (key_pos >= begin) & (key_pos < end)
            bias[slot * block_len:(slot + 1) * block_len, :] = jnp.where(inside, 0.0, NEG)

    low_half = lane_group((chunk, LANES), LANES // 2) == 0
    half_lane = lane_group((HEADS, LANES), LANES // 2)
    pick_row = lax.broadcasted_iota(jnp.int32, (HEADS, LANES), 0)
    pick_lane = lax.broadcasted_iota(jnp.int32, (HEADS, LANES), 1)
    steps = [(index, head) for index in range(chunks) for head in range(HEADS)]
    scores, softs, mixes, log_high, log_low = {}, {}, {}, {}, {}
    moves = []
    for turn in range(len(steps) + 4):
        if turn < len(steps):
            index, head = steps[turn]
            pair, half = divmod(head, 2)
            if head == 0:
                make_bias(index)
            if index == 0 and half == 0:
                copies[pair].wait()
            span = slice(index * group, (index + 1) * group)
            rows = recv[span, pair * pair_rows:(pair + 1) * pair_rows, :].reshape(chunk, LANES)
            keys = table[pair, 2 * key_count:, half * LANES:(half + 1) * LANES]
            scores[turn] = mm_nt(rows, keys) + bias[index * chunk:(index + 1) * chunk, :]
        item = scores.pop(turn - 2, None)
        if item is not None:
            top = jnp.max(item, axis=-1, keepdims=True)
            softs[turn - 2] = (top, jnp.exp2(item - top).astype(jnp.bfloat16))
        step = turn - 4
        if step < 0:
            continue
        index, head = steps[step]
        pair, half = divmod(head, 2)
        mixes[step] = mm(softs[step][1], table[pair, half * key_count:(half + 1) * key_count, :])
        if half == 0:
            continue
        mixed = mixes.pop(step - 1) + mixes.pop(step)
        total = mixed[:, LANES:]
        span = slice(index * group, (index + 1) * group)
        part = slice(pair * pair_rows, (pair + 1) * pair_rows)
        back[span, part, :] = (mixed[:, :LANES] / total).astype(jnp.bfloat16).reshape(group, pair_rows, LANES)
        logs = jnp.where(low_half, softs.pop(step - 1)[0], softs.pop(step)[0]) + jnp.log2(total)
        high = logs.astype(jnp.bfloat16)
        low = (logs - high.astype(jnp.float32)).astype(jnp.bfloat16)
        pick = (
            ((pick_row == 2 * pair) & (pick_lane == 0)) | ((pick_row == 2 * pair + 1) & (pick_lane == LANES // 2))
        ).astype(jnp.float32).astype(jnp.bfloat16)
        log_high[index] = mm_nt(pick, high) + log_high.get(index, 0.0)
        log_low[index] = mm_nt(pick, low) + log_low.get(index, 0.0)
        if pair < pairs - 1:
            continue
        for offset in range(group):
            lane = offset * pair_rows
            tile, shift = lane // LANES, lane % LANES
            high = log_high[index][:, tile * LANES:(tile + 1) * LANES]
            low = log_low[index][:, tile * LANES:(tile + 1) * LANES]
            if shift:
                high = pltpu.roll(high, LANES - shift, 1)
            low_shift = (LANES // 2 - shift) % LANES
            if low_shift:
                low = pltpu.roll(low, low_shift, 1)
            back[index * group + offset, pairs * pair_rows:pairs * pair_rows + HEADS, :] = jnp.where(
                half_lane == 0, high, low
            ).astype(jnp.bfloat16)
        place = pl.ds(index * group, group)
        moves.append(pltpu.make_async_copy(back.at[place], back_h.at[place], outs.at[index]))
        moves[-1].start()
    for item in moves:
        item.wait()


def combine_kernel(block_len, capacity, routes_h, ranks_h, back, attended, routes, ranks, logs, sems):
    node_count, message_rows, _ = back.shape
    width = attended.shape[1]
    pairs = width // LANES
    pair_rows = capacity * block_len
    copies = fetch([(routes_h, routes), (ranks_h, ranks)], sems)
    route_count, block_count = routes.shape
    halves = back[:, pairs * pair_rows:pairs * pair_rows + HEADS, :].astype(jnp.float32).reshape(node_count * HEADS, LANES)
    logs[...] = halves + pltpu.roll(halves, LANES // 2, 1)
    for item in copies:
        item.wait()
    group = lane_group((HEADS, LANES), block_len)
    per_tile = LANES // block_len
    tiles = block_count // per_tile
    route_logs = []
    for route in range(route_count):
        parts = []
        for tile in range(tiles):
            gathered = jnp.zeros((HEADS, LANES), jnp.float32)
            for spot in range(per_tile):
                block = tile * per_tile + spot
                start = pl.multiple_of(routes[route, block] * HEADS, HEADS)
                shift = (spot + per_tile - ranks[route, block]) * block_len % LANES
                moved = pltpu.roll(logs[pl.ds(start, HEADS), :], shift, 1)
                gathered = jnp.where(group == spot, moved, gathered)
            parts.append(gathered)
        route_logs.append(jnp.concatenate(parts, axis=1))
    best = functools.reduce(jnp.maximum, route_logs)
    terms = [jnp.exp2(item - best) for item in route_logs]
    total = functools.reduce(jnp.add, terms)
    spread = (
        lax.broadcasted_iota(jnp.int32, (2 * HEADS, width), 1) // (width // HEADS)
        == lax.broadcasted_iota(jnp.int32, (2 * HEADS, width), 0) % HEADS
    ).astype(jnp.float32).astype(jnp.bfloat16)
    weights = []
    for item in terms:
        share = item / total
        high = share.astype(jnp.bfloat16).astype(jnp.float32)
        both = jnp.concatenate([high, share - high], axis=0).astype(jnp.bfloat16)
        weights.append(mm_tn(both, spread))
    for block in range(block_count):
        rows = slice(block * block_len, (block + 1) * block_len)
        for pair in range(pairs):
            lanes = slice(pair * LANES, (pair + 1) * LANES)
            acc = None
            for route in range(route_count):
                start = pl.multiple_of(pair * pair_rows + ranks[route, block] * block_len, block_len)
                piece = back[routes[route, block], pl.ds(start, block_len), :].astype(jnp.float32)
                piece = piece * weights[route][rows, lanes]
                acc = piece if acc is None else acc + piece
            attended[rows, lanes] = acc.astype(jnp.bfloat16)


def own_kernel(query_scale, mesh_h, attended, w_out_h, w_qkv_h, encoded, own, mixes, tops, mesh, w_out, w_qkv, sems):
    copies = fetch([(w_out_h, w_out), (mesh_h, mesh), (w_qkv_h, w_qkv)], sems)
    width = attended.shape[1]
    for item in copies[:2]:
        item.wait()
    rows = (mesh[...].astype(jnp.float32) + mm(attended[...], w_out[...])).astype(jnp.bfloat16)
    encoded[...] = rows
    own[:, width:] = rows
    normed = norm_rows(rows)
    copies[2].wait()
    query = (mm(normed, w_qkv[:, :width]) * query_scale).astype(jnp.bfloat16)
    own[:, :width] = query
    keyval = mm(normed, w_qkv[:, width:]).astype(jnp.bfloat16)
    low_half = lane_group((rows.shape[0], LANES), LANES // 2) == 0
    masks = half_masks()
    scores, softs, mixed = {}, {}, {}
    for turn in range(HEADS + 2):
        if turn < HEADS:
            lanes = slice(turn // 2 * LANES, (turn // 2 + 1) * LANES)
            scores[turn] = mm_nt(query[:, lanes], keyval[:, lanes] * masks[turn % 2])
        head = turn - 1
        if 0 <= head < HEADS:
            item = scores.pop(head)
            top = jnp.max(item, axis=-1, keepdims=True)
            softs[head] = (top, jnp.exp2(item - top).astype(jnp.bfloat16))
        head = turn - 2
        if head < 0:
            continue
        pair, half = divmod(head, 2)
        value = keyval[:, width + pair * LANES:width + (pair + 1) * LANES]
        table = jnp.concatenate([value * masks[half], jnp.broadcast_to(masks[half], value.shape)], axis=1)
        mixed[half] = mm(softs[head][1], table)
        if half:
            mixes[pair] = mixed[0] + mixed[1]
            tops[pair] = jnp.where(low_half, softs.pop(head - 1)[0], softs.pop(head)[0])


def window_kernel(edges, own, mixes, tops, mesh_prev, mesh_next, att_prev, att_next, w_out_h, w_qkv_h, w_proc_h,
                  processed, w_out, w_near, w_proc, mixed, sems):
    rows, width = mixed.shape
    copies = fetch([(w_out_h, w_out), (w_qkv_h.at[:, pl.ds(width, 2 * width)], w_near), (w_proc_h, w_proc)], sems)
    mesh_both = jnp.concatenate([mesh_prev[...], mesh_next[...]], axis=0)
    att_both = jnp.concatenate([att_prev[...], att_next[...]], axis=0)
    copies[0].wait()
    near = (mesh_both.astype(jnp.float32) + mm(att_both, w_out[...])).astype(jnp.bfloat16)
    normed = norm_rows(near)
    copies[1].wait()
    near_kv = mm(normed, w_near[...]).astype(jnp.bfloat16)
    behind = lax.broadcasted_iota(jnp.int32, (rows, rows), 1) >= lax.broadcasted_iota(jnp.int32, (rows, rows), 0)
    behind_f = behind.astype(jnp.float32)
    bias = behind_f * jnp.where(edges[0] > 0, 0.0, NEG) + (1.0 - behind_f) * jnp.where(edges[1] > 0, 0.0, NEG)
    low_half = lane_group((rows, LANES), LANES // 2) == 0
    masks = half_masks()
    scores, softs, sums = {}, {}, {}
    for turn in range(HEADS + 2):
        if turn < HEADS:
            lanes = slice(turn // 2 * LANES, (turn // 2 + 1) * LANES)
            both = mm_nt(own[:, lanes], near_kv[:, lanes] * masks[turn % 2])
            scores[turn] = jnp.where(behind, both[:, :rows], both[:, rows:]) + bias
        head = turn - 1
        if 0 <= head < HEADS:
            item = scores.pop(head)
            top = jnp.max(item, axis=-1, keepdims=True)
            term = jnp.exp2(item - top)
            first = jnp.where(behind, term, 0.0)
            softs[head] = (top, jnp.concatenate([first, term - first], axis=1).astype(jnp.bfloat16))
        head = turn - 2
        if head < 0:
            continue
        pair, half = divmod(head, 2)
        value = near_kv[:, width + pair * LANES:width + (pair + 1) * LANES]
        table = jnp.concatenate([value * masks[half], jnp.broadcast_to(masks[half], value.shape)], axis=1)
        sums[half] = mm(softs[head][1], table)
        if half:
            top = jnp.where(low_half, softs.pop(head - 1)[0], softs.pop(head)[0])
            best = jnp.maximum(top, tops[pair])
            near_part, own_part = jnp.exp2(top - best), jnp.exp2(tops[pair] - best)
            total = sums[0] + sums[1]
            share = total[:, :LANES] * near_part + mixes[pair, :, :LANES] * own_part
            count = total[:, LANES:] * near_part + mixes[pair, :, LANES:] * own_part
            mixed[:, pair * LANES:(pair + 1) * LANES] = (share / count).astype(jnp.bfloat16)
    copies[2].wait()
    processed[...] = (own[:, width:].astype(jnp.float32) + mm(mixed[...], w_proc[...])).astype(jnp.bfloat16)


def call(kernel, name, outs, out_specs, operands, scratch, cost, limit=LIMIT, near=()):
    return pl.pallas_call(
        kernel,
        name=name,
        out_shape=outs,
        in_specs=[SMEM if item.shape == (2,) else VMEM if i in near else ANY for i, item in enumerate(operands)],
        out_specs=out_specs,
        scratch_shapes=scratch,
        cost_estimate=pl.CostEstimate(flops=cost[0], bytes_accessed=cost[1], transcendentals=cost[2]),
        compiler_params=pltpu.CompilerParams(vmem_limit_bytes=limit),
    )(*operands)


def shape(dims, dtype=jnp.bfloat16):
    return jax.ShapeDtypeStruct(dims, dtype)


def held(item):
    return pltpu.VMEM(item.shape, item.dtype)


def dma(count):
    return pltpu.SemaphoreType.DMA((count,))


def local(grid_feats, mesh_feats, routes, edge_first, edge_count, w_query, w_kv, w_out_enc, w_qkv, w_out_proc):
    width = w_query.shape[1]
    model = mesh_feats.shape[1]
    query_scale = math.log2(math.e) / math.sqrt(width // HEADS)
    node_count = lax.axis_size("outer") * lax.axis_size("inner")
    block_count, route_count = routes.shape
    rows = mesh_feats.shape[0]
    key_count = grid_feats.shape[0]
    block_len = rows // block_count
    capacity = max(1, (block_count * route_count + node_count - 1) // node_count)
    pairs = width // LANES
    pair_rows = capacity * block_len
    note_rows = max(8, -(-2 * capacity // 8) * 8)
    message = shape((node_count, pairs * pair_rows + note_rows, LANES))
    message_bytes = 2 * math.prod(message.shape)
    routes_t, first_t, count_t = routes.T, edge_first.T, edge_count.T
    ranks_shape = shape(routes_t.shape, jnp.int32)
    in_smem = pltpu.SMEM(routes_t.shape, jnp.int32)
    place = (block_len, capacity)

    send, ranks = call(
        functools.partial(send_kernel, *place, query_scale),
        "send_queries",
        [message, ranks_shape],
        [VMEM, SMEM],
        (routes_t, first_t, count_t, mesh_feats, w_query),
        [in_smem, held(first_t), held(count_t), held(mesh_feats), held(w_query), pltpu.SMEM((node_count,), jnp.int32),
         pltpu.VMEM((node_count * note_rows, LANES), jnp.float32), dma(5)],
        (2 * rows * model * width, 2 * model * (rows + width) + message_bytes, 0),
        None,
    )
    recv = lax.all_to_all(send, AXES, split_axis=0, concat_axis=0, tiled=True)

    table = call(
        grid_kernel,
        "grid_keys",
        shape((pairs, 3 * key_count, 2 * LANES)),
        VMEM,
        (grid_feats, w_kv),
        [held(grid_feats), held(w_kv), dma(2)],
        (4 * key_count * model * width, 2 * model * (key_count + 2 * width) + 12 * key_count * width, 0),
        None,
    )

    forward = [(i, i + 1) for i in range(node_count - 1)]
    backward = [(i + 1, i) for i in range(node_count - 1)]
    late_mesh, table = lax.optimization_barrier((mesh_feats, table))
    mesh_prev = lax.ppermute(late_mesh, AXES, forward)
    mesh_next = lax.ppermute(late_mesh, AXES, backward)

    chunk = math.gcd(node_count * pair_rows, 512)
    back = call(
        functools.partial(owner_kernel, *place, chunk),
        "owner_attention",
        message,
        HBM,
        (recv, table),
        [held(table), held(message), pltpu.VMEM((node_count * pair_rows, key_count), jnp.float32), dma(pairs),
         dma(node_count * pair_rows // chunk)],
        (4 * node_count * pair_rows * key_count * width, 2 * message_bytes, node_count * pair_rows * key_count * HEADS),
        near=(0,),
    )
    back = lax.all_to_all(back, AXES, split_axis=0, concat_axis=0, tiled=True)

    attended = call(
        functools.partial(combine_kernel, *place),
        "combine_routes",
        shape((rows, width)),
        VMEM,
        (routes_t, ranks, back),
        [in_smem, in_smem, pltpu.VMEM((node_count * HEADS, LANES), jnp.float32), dma(2)],
        (4 * rows * width * route_count, message_bytes, 0),
        near=(2,),
    )
    att_prev = lax.ppermute(attended, AXES, forward)
    att_next = lax.ppermute(attended, AXES, backward)

    encoded, own, mixes, tops = call(
        functools.partial(own_kernel, query_scale),
        "own_rows",
        [shape((rows, model)), shape((rows, width + model)), shape((pairs, rows, 2 * LANES), jnp.float32),
         shape((pairs, rows, LANES), jnp.float32)],
        [VMEM] * 4,
        (mesh_feats, attended, w_out_enc, w_qkv),
        [held(mesh_feats), held(w_out_enc), held(w_qkv), dma(3)],
        (8 * rows * model * width, 2 * model * (2 * rows + 4 * width), 0),
        near=(1,),
    )

    place_index = lax.axis_index(AXES)
    edges = jnp.stack([place_index > 0, place_index < node_count - 1]).astype(jnp.int32)
    processed = call(
        window_kernel,
        "window_attention",
        shape((rows, model)),
        VMEM,
        (edges, own, mixes, tops, mesh_prev, mesh_next, att_prev, att_next, w_out_enc, w_qkv, w_out_proc),
        [held(w_out_enc), pltpu.VMEM((model, 2 * width), jnp.bfloat16), held(w_out_proc),
         pltpu.VMEM((rows, width), jnp.bfloat16), dma(3)],
        (16 * rows * model * width, 2 * model * (4 * rows + 5 * width), 3 * rows * rows * HEADS),
        near=range(1, 8),
    )
    return (encoded, processed)


def solution(mesh):
    rows = P(("groups", "outer", "inner"), None)
    return jax.shard_map(
        local,
        mesh=mesh,
        in_specs=(rows,) * 5 + (P(),) * 5,
        out_specs=(rows, rows),
        check_vma=False,
    )
```

```python
import functools
import math

import jax
import jax.numpy as jnp
from jax import lax
from jax.experimental import pallas as pl
from jax.experimental.pallas import tpu as pltpu
from jax.sharding import PartitionSpec as P


HEADS = 8
LANES = 128
NEG = -1e30
AXES = ("outer", "inner")
VMEM = pl.BlockSpec(memory_space=pltpu.VMEM)
SMEM = pl.BlockSpec(memory_space=pltpu.SMEM)
ANY = pl.BlockSpec(memory_space=pl.ANY)
HBM = pl.BlockSpec(memory_space=pltpu.HBM)
LIMIT = 50 << 20


def norm_rows(inputs):
    as_float = inputs.astype(jnp.float32)
    row_mean = jnp.mean(as_float, axis=-1, keepdims=True)
    centered = as_float - row_mean
    variance = jnp.mean(centered * centered, axis=-1, keepdims=True)
    return (centered * lax.rsqrt(variance + 1e-05)).astype(jnp.bfloat16)


def mm(a, b):
    return jnp.dot(a, b, preferred_element_type=jnp.float32)


def mm_nt(a, b):
    return lax.dot_general(a, b, (((1,), (1,)), ((), ())), preferred_element_type=jnp.float32)


def mm_tn(a, b):
    return lax.dot_general(a, b, (((0,), (0,)), ((), ())), preferred_element_type=jnp.float32)


def lane_group(shape, width):
    return lax.broadcasted_iota(jnp.int32, shape, len(shape) - 1) // width


def half_masks():
    low = (lane_group((1, LANES), LANES // 2) == 0).astype(jnp.float32)
    return low.astype(jnp.bfloat16), (1.0 - low).astype(jnp.bfloat16)


def fetch(pairs, sems):
    copies = [pltpu.make_async_copy(src, dst, sems.at[i]) for i, (src, dst) in enumerate(pairs)]
    for item in copies:
        item.start()
    return copies


def send_kernel(block_len, capacity, query_scale, routes_h, first_h, count_h, mesh_h, w_query_h, send, ranks,
                routes, first, count, mesh, w_query, tally, notes, sems):
    copies = fetch(
        [(mesh_h, mesh), (w_query_h, w_query), (routes_h, routes), (first_h, first), (count_h, count)], sems
    )
    route_count, block_count = routes.shape
    node_count = send.shape[0]
    pair_rows = capacity * block_len
    pairs = w_query.shape[1] // LANES
    note_rows = send.shape[1] - pairs * pair_rows

    def clear(i, carry):
        tally[i] = 0
        return carry

    lax.fori_loop(0, node_count, clear, 0)
    if node_count * capacity != block_count * route_count:
        send[...] = jnp.zeros(send.shape, send.dtype)
    notes[...] = jnp.zeros(notes.shape, notes.dtype)
    copies[0].wait()
    normed = norm_rows(mesh[...])
    for item in copies[1:]:
        item.wait()
    first_all = first[...]
    upper = first_all >= 256
    low_part = jnp.where(upper, first_all - 256, first_all).astype(jnp.float32)
    signed = jnp.where(upper, -count[...], count[...]).astype(jnp.float32)
    group = lane_group((1, LANES), block_len)
    per_tile = LANES // block_len
    queries = (mm(normed, w_query[...]) * query_scale).astype(jnp.bfloat16)
    for block in range(block_count):
        tile, spot = divmod(block, per_tile)
        cols = slice(tile * LANES, (tile + 1) * LANES)
        rows = slice(block * block_len, (block + 1) * block_len)
        for route in range(route_count):
            owner = routes[route, block]
            rank = tally[owner]
            tally[owner] = rank + 1
            ranks[route, block] = rank
            for pair in range(pairs):
                start = pl.multiple_of(pair * pair_rows + rank * block_len, block_len)
                send[owner, pl.ds(start, block_len), :] = queries[rows, pair * LANES:(pair + 1) * LANES]
            note = owner * note_rows + 2 * rank
            keep = group == spot
            notes[pl.ds(note, 1), :] = jnp.where(keep, low_part[route:route + 1, cols], 0.0)
            notes[pl.ds(note + 1, 1), :] = jnp.where(keep, signed[route:route + 1, cols], 0.0)
    for owner in range(node_count):
        send[owner, pairs * pair_rows:, :] = notes[owner * note_rows:(owner + 1) * note_rows, :].astype(jnp.bfloat16)


def grid_kernel(grid_h, w_kv_h, table, grid, w_kv, sems):
    copies = fetch([(grid_h, grid), (w_kv_h, w_kv)], sems)
    width = w_kv.shape[1] // 2
    copies[0].wait()
    normed = norm_rows(grid[...])
    copies[1].wait()
    grid_kv = mm(normed, w_kv[...]).astype(jnp.bfloat16)
    count = grid_kv.shape[0]
    masks = half_masks()
    for pair in range(width // LANES):
        key_pair = grid_kv[:, pair * LANES:(pair + 1) * LANES]
        value_pair = grid_kv[:, width + pair * LANES:width + (pair + 1) * LANES]
        for half in range(2):
            mask = masks[half]
            rows = slice(half * count, (half + 1) * count)
            table[pair, rows, :LANES] = value_pair * mask
            table[pair, rows, LANES:] = jnp.broadcast_to(mask, (count, LANES))
            table[pair, 2 * count:, half * LANES:(half + 1) * LANES] = key_pair * mask


def owner_kernel(block_len, capacity, chunk, recv, table_h, back_h, table, back, bias, sems, outs):
    node_count, message_rows, _ = recv.shape
    pairs, table_rows, _ = table.shape
    key_count = table_rows // 3
    pair_rows = capacity * block_len
    note_rows = message_rows - pairs * pair_rows
    group = chunk // pair_rows
    chunks = node_count // group
    copies = fetch([(table_h.at[pair], table.at[pair]) for pair in range(pairs)], sems)
    tags = recv[:, pairs * pair_rows:, :].reshape(node_count * note_rows, LANES)
    fold = (
        lax.broadcasted_iota(jnp.int32, (block_len, LANES), 1) % block_len
        == lax.broadcasted_iota(jnp.int32, (block_len, LANES), 0)
    ).astype(jnp.float32).astype(jnp.bfloat16)
    columns = mm_nt(fold, tags)
    key_pos = lax.broadcasted_iota(jnp.int32, (block_len, key_count), 1).astype(jnp.float32)

    def make_bias(index):
        for slot in range(index * group * capacity, (index + 1) * group * capacity):
            spot = slot // capacity * note_rows + 2 * (slot % capacity)
            low_part, signed = columns[:, spot:spot + 1], columns[:, spot + 1:spot + 2]
            begin = low_part + jnp.where(signed < 0, 256.0, 0.0)
            end = begin + jnp.maximum(jnp.abs(signed), 1.0)
            inside = (key_pos >= begin) & (key_pos < end)
            bias[slot * block_len:(slot + 1) * block_len, :] = jnp.where(inside, 0.0, NEG)

    low_half = lane_group((chunk, LANES), LANES // 2) == 0
    half_lane = lane_group((HEADS, LANES), LANES // 2)
    log_width = LANES // 2 // pairs
    log_group = lane_group((chunk, LANES), log_width) % pairs
    pick_row = lax.broadcasted_iota(jnp.int32, (HEADS, LANES), 0)
    pick_lane = lax.broadcasted_iota(jnp.int32, (HEADS, LANES), 1)
    pick = (pick_lane == pick_row % 2 * (LANES // 2) + pick_row // 2 * log_width).astype(jnp.float32).astype(jnp.bfloat16)
    steps = [(index, head) for index in range(chunks) for head in range(HEADS)]
    scores, softs, mixes, held_logs = {}, {}, {}, {}
    moves = []
    for turn in range(len(steps) + 4):
        if turn < len(steps):
            index, head = steps[turn]
            pair, half = divmod(head, 2)
            if head == 0:
                make_bias(index)
            if index == 0 and half == 0:
                copies[pair].wait()
            span = slice(index * group, (index + 1) * group)
            rows = recv[span, pair * pair_rows:(pair + 1) * pair_rows, :].reshape(chunk, LANES)
            keys = table[pair, 2 * key_count:, half * LANES:(half + 1) * LANES]
            scores[turn] = mm_nt(rows, keys) + bias[index * chunk:(index + 1) * chunk, :]
        item = scores.pop(turn - 2, None)
        if item is not None:
            top = jnp.max(item, axis=-1, keepdims=True)
            softs[turn - 2] = (top, jnp.exp2(item - top).astype(jnp.bfloat16))
        step = turn - 4
        if step < 0:
            continue
        index, head = steps[step]
        pair, half = divmod(head, 2)
        mixes[step] = mm(softs[step][1], table[pair, half * key_count:(half + 1) * key_count, :])
        if half == 0:
            continue
        mixed = mixes.pop(step - 1) + mixes.pop(step)
        total = mixed[:, LANES:]
        span = slice(index * group, (index + 1) * group)
        part = slice(pair * pair_rows, (pair + 1) * pair_rows)
        back[span, part, :] = (mixed[:, :LANES] / total).astype(jnp.bfloat16).reshape(group, pair_rows, LANES)
        logs = jnp.where(low_half, softs.pop(step - 1)[0], softs.pop(step)[0]) + jnp.log2(total)
        held_logs[index] = jnp.where(log_group == pair, logs, held_logs[index]) if pair else logs
        if pair < pairs - 1:
            continue
        logs = held_logs.pop(index)
        high = logs.astype(jnp.bfloat16)
        log_high = mm_nt(pick, high)
        log_low = mm_nt(pick, (logs - high.astype(jnp.float32)).astype(jnp.bfloat16))
        for offset in range(group):
            lane = offset * pair_rows
            tile, shift = lane // LANES, lane % LANES
            high = log_high[:, tile * LANES:(tile + 1) * LANES]
            low = log_low[:, tile * LANES:(tile + 1) * LANES]
            if shift:
                high = pltpu.roll(high, LANES - shift, 1)
            low_shift = (LANES // 2 - shift) % LANES
            if low_shift:
                low = pltpu.roll(low, low_shift, 1)
            back[index * group + offset, pairs * pair_rows:pairs * pair_rows + HEADS, :] = jnp.where(
                half_lane == 0, high, low
            ).astype(jnp.bfloat16)
        place = pl.ds(index * group, group)
        moves.append(pltpu.make_async_copy(back.at[place], back_h.at[place], outs.at[index]))
        moves[-1].start()
    for item in moves:
        item.wait()


def combine_kernel(block_len, capacity, routes_h, ranks_h, back, attended, routes, ranks, logs, sems):
    node_count, _, _ = back.shape
    width = attended.shape[1]
    pairs = width // LANES
    pair_rows = capacity * block_len
    copies = fetch([(routes_h, routes), (ranks_h, ranks)], sems)
    route_count, block_count = routes.shape
    halves = back[:, pairs * pair_rows:pairs * pair_rows + HEADS, :].astype(jnp.float32).reshape(node_count * HEADS, LANES)
    logs[...] = halves + pltpu.roll(halves, LANES // 2, 1)
    for item in copies:
        item.wait()
    group = lane_group((HEADS, LANES), block_len)
    per_tile = LANES // block_len
    tiles = block_count // per_tile
    route_logs = []
    for route in range(route_count):
        parts = []
        for tile in range(tiles):
            gathered = jnp.zeros((HEADS, LANES), jnp.float32)
            for spot in range(per_tile):
                block = tile * per_tile + spot
                start = pl.multiple_of(routes[route, block] * HEADS, HEADS)
                shift = (spot + per_tile - ranks[route, block]) * block_len % LANES
                moved = pltpu.roll(logs[pl.ds(start, HEADS), :], shift, 1)
                gathered = jnp.where(group == spot, moved, gathered)
            parts.append(gathered)
        route_logs.append(jnp.concatenate(parts, axis=1))
    best = functools.reduce(jnp.maximum, route_logs)
    terms = [jnp.exp2(item - best) for item in route_logs]
    total = functools.reduce(jnp.add, terms)
    spread = (
        lax.broadcasted_iota(jnp.int32, (2 * HEADS, width), 1) // (width // HEADS)
        == lax.broadcasted_iota(jnp.int32, (2 * HEADS, width), 0) % HEADS
    ).astype(jnp.float32).astype(jnp.bfloat16)
    weights = []
    for item in terms:
        share = item / total
        high = share.astype(jnp.bfloat16).astype(jnp.float32)
        both = jnp.concatenate([high, share - high], axis=0).astype(jnp.bfloat16)
        weights.append(mm_tn(both, spread))
    for block in range(block_count):
        rows = slice(block * block_len, (block + 1) * block_len)
        for pair in range(pairs):
            lanes = slice(pair * LANES, (pair + 1) * LANES)
            acc = None
            for route in range(route_count):
                start = pl.multiple_of(pair * pair_rows + ranks[route, block] * block_len, block_len)
                piece = back[routes[route, block], pl.ds(start, block_len), :].astype(jnp.float32)
                piece = piece * weights[route][rows, lanes]
                acc = piece if acc is None else acc + piece
            attended[rows, lanes] = acc.astype(jnp.bfloat16)


def own_kernel(query_scale, mesh_h, attended, w_out_h, w_qkv_h, encoded, own, keyval, mixes,
               mesh, w_out, w_qkv, sems):
    copies = fetch([(w_out_h, w_out), (mesh_h, mesh), (w_qkv_h, w_qkv)], sems)
    width = attended.shape[1]
    for item in copies[:2]:
        item.wait()
    rows = (mesh[...].astype(jnp.float32) + mm(attended[...], w_out[...])).astype(jnp.bfloat16)
    encoded[...] = rows
    own[:, width:] = rows
    normed = norm_rows(rows)
    copies[2].wait()
    query = (mm(normed, w_qkv[:, :width]) * query_scale).astype(jnp.bfloat16)
    own[:, :width] = query
    keyval[...] = mm(normed, w_qkv[:, width:]).astype(jnp.bfloat16)
    low_half = lane_group((rows.shape[0], LANES), LANES // 2) == 0
    masks = half_masks()
    scores, softs, mixed = {}, {}, {}
    for turn in range(HEADS + 2):
        if turn < HEADS:
            lanes = slice(turn // 2 * LANES, (turn // 2 + 1) * LANES)
            scores[turn] = mm_nt(query[:, lanes], keyval[:, lanes] * masks[turn % 2])
        head = turn - 1
        if 0 <= head < HEADS:
            item = scores.pop(head)
            top = jnp.max(item, axis=-1, keepdims=True)
            softs[head] = (top, jnp.exp2(item - top).astype(jnp.bfloat16))
        head = turn - 2
        if head < 0:
            continue
        pair, half = divmod(head, 2)
        value = keyval[:, width + pair * LANES:width + (pair + 1) * LANES]
        table = jnp.concatenate([value * masks[half], jnp.broadcast_to(masks[half], value.shape)], axis=1)
        mixed[half] = mm(softs[head][1], table)
        if half:
            total = mixed[0] + mixed[1]
            mixes[pair, :, :LANES] = total[:, :LANES] / total[:, LANES:]
            top = jnp.where(low_half, softs.pop(head - 1)[0], softs.pop(head)[0])
            mixes[pair, :, LANES:] = top + jnp.log2(total[:, LANES:])


def window_kernel(edges, own, mixes, mesh_far, att_far, chip_kv_h, w_out_h, w_qkv_h, w_proc_h, processed,
                  chip_kv, w_out, w_near, w_proc, mixed, sems):
    rows, width = mixed.shape
    copies = fetch(
        [
            (w_out_h, w_out),
            (w_qkv_h.at[:, pl.ds(width, 2 * width)], w_near),
            (chip_kv_h, chip_kv),
            (w_proc_h, w_proc),
        ],
        sems,
    )
    copies[0].wait()
    far = (mesh_far[...].astype(jnp.float32) + mm(att_far[...], w_out[...])).astype(jnp.bfloat16)
    normed = norm_rows(far)
    copies[1].wait()
    far_kv = mm(normed, w_near[...]).astype(jnp.bfloat16)
    copies[2].wait()
    behind = lax.broadcasted_iota(jnp.int32, (rows, rows), 1) >= lax.broadcasted_iota(jnp.int32, (rows, rows), 0)
    in_far = behind.astype(jnp.int32) != edges[0]
    bias = jnp.where(in_far & (edges[1] == 0), NEG, 0.0)
    low_half = lane_group((rows, LANES), LANES // 2) == 0
    masks = half_masks()
    scores, softs, sums = {}, {}, {}
    for turn in range(HEADS + 2):
        if turn < HEADS:
            lanes = slice(turn // 2 * LANES, (turn // 2 + 1) * LANES)
            mask = masks[turn % 2]
            far_scores = mm_nt(own[:, lanes], far_kv[:, lanes] * mask)
            chip_scores = mm_nt(own[:, lanes], chip_kv[:, lanes] * mask)
            scores[turn] = jnp.where(in_far, far_scores, chip_scores) + bias
        head = turn - 1
        if 0 <= head < HEADS:
            item = scores.pop(head)
            top = jnp.max(item, axis=-1, keepdims=True)
            term = jnp.exp2(item - top)
            first = jnp.where(in_far, term, 0.0)
            softs[head] = (top, jnp.concatenate([first, term - first], axis=1).astype(jnp.bfloat16))
        head = turn - 2
        if head < 0:
            continue
        pair, half = divmod(head, 2)
        lanes = slice(width + pair * LANES, width + (pair + 1) * LANES)
        value = jnp.concatenate([far_kv[:, lanes], chip_kv[:, lanes]], axis=0)
        table = jnp.concatenate([value * masks[half], jnp.broadcast_to(masks[half], value.shape)], axis=1)
        sums[half] = mm(softs[head][1], table)
        if half:
            top = jnp.where(low_half, softs.pop(head - 1)[0], softs.pop(head)[0])
            own_log = mixes[pair, :, LANES:]
            best = jnp.maximum(top, own_log)
            near_part, own_part = jnp.exp2(top - best), jnp.exp2(own_log - best)
            total = sums[0] + sums[1]
            share = total[:, :LANES] * near_part + mixes[pair, :, :LANES] * own_part
            count = total[:, LANES:] * near_part + own_part
            mixed[:, pair * LANES:(pair + 1) * LANES] = (share / count).astype(jnp.bfloat16)
    copies[3].wait()
    processed[...] = (own[:, width:].astype(jnp.float32) + mm(mixed[...], w_proc[...])).astype(jnp.bfloat16)


def call(kernel, outs, out_specs, operands, scratch, cost, limit=LIMIT, near=()):
    return pl.pallas_call(
        kernel,
        out_shape=outs,
        in_specs=[SMEM if item.shape == (2,) else VMEM if i in near else ANY for i, item in enumerate(operands)],
        out_specs=out_specs,
        scratch_shapes=scratch,
        cost_estimate=pl.CostEstimate(flops=cost[0], bytes_accessed=cost[1], transcendentals=cost[2]),
        compiler_params=pltpu.CompilerParams(vmem_limit_bytes=limit),
    )(*operands)


def shape(dims, dtype=jnp.bfloat16):
    return jax.ShapeDtypeStruct(dims, dtype)


def held(item):
    return pltpu.VMEM(item.shape, item.dtype)


def dma(count):
    return pltpu.SemaphoreType.DMA((count,))


def local(grid_feats, mesh_feats, routes, edge_first, edge_count, w_query, w_kv, w_out_enc, w_qkv, w_out_proc):
    width = w_query.shape[1]
    model = mesh_feats.shape[1]
    query_scale = math.log2(math.e) / math.sqrt(width // HEADS)
    node_count = lax.axis_size("outer") * lax.axis_size("inner")
    block_count, route_count = routes.shape
    rows = mesh_feats.shape[0]
    key_count = grid_feats.shape[0]
    block_len = rows // block_count
    capacity = max(1, (block_count * route_count + node_count - 1) // node_count)
    pairs = width // LANES
    pair_rows = capacity * block_len
    note_rows = max(8, -(-2 * capacity // 8) * 8)
    message = shape((node_count, pairs * pair_rows + note_rows, LANES))
    message_bytes = 2 * math.prod(message.shape)
    routes_t, first_t, count_t = routes.T, edge_first.T, edge_count.T
    ranks_shape = shape(routes_t.shape, jnp.int32)
    in_smem = pltpu.SMEM(routes_t.shape, jnp.int32)
    place = (block_len, capacity)

    send, ranks = call(
        functools.partial(send_kernel, *place, query_scale),
        [message, ranks_shape],
        [VMEM, SMEM],
        (routes_t, first_t, count_t, mesh_feats, w_query),
        [in_smem, held(first_t), held(count_t), held(mesh_feats), held(w_query), pltpu.SMEM((node_count,), jnp.int32),
         pltpu.VMEM((node_count * note_rows, LANES), jnp.float32), dma(5)],
        (2 * rows * model * width, 2 * model * (rows + width) + message_bytes, 0),
        None,
    )
    recv = lax.all_to_all(send, AXES, split_axis=0, concat_axis=0, tiled=True)

    table = call(
        grid_kernel,
        shape((pairs, 3 * key_count, 2 * LANES)),
        VMEM,
        (grid_feats, w_kv),
        [held(grid_feats), held(w_kv), dma(2)],
        (4 * key_count * model * width, 2 * model * (key_count + 2 * width) + 12 * key_count * width, 0),
        None,
    )

    on_chip = [(i, i ^ 1) for i in range(node_count)]
    off_chip = [(i, i + 1) for i in range(1, node_count - 1, 2)] + [(i + 1, i) for i in range(1, node_count - 1, 2)]
    late_mesh, table = lax.optimization_barrier((mesh_feats, table))
    mesh_far = lax.ppermute(late_mesh, AXES, off_chip)

    chunk = math.gcd(node_count * pair_rows, 512)
    back = call(
        functools.partial(owner_kernel, *place, chunk),
        message,
        HBM,
        (recv, table),
        [held(table), held(message), pltpu.VMEM((node_count * pair_rows, key_count), jnp.float32), dma(pairs),
         dma(node_count * pair_rows // chunk)],
        (4 * node_count * pair_rows * key_count * width, 2 * message_bytes, node_count * pair_rows * key_count * HEADS),
        near=(0,),
    )
    back = lax.all_to_all(back, AXES, split_axis=0, concat_axis=0, tiled=True)

    attended = call(
        functools.partial(combine_kernel, *place),
        shape((rows, width)),
        VMEM,
        (routes_t, ranks, back),
        [in_smem, in_smem, pltpu.VMEM((node_count * HEADS, LANES), jnp.float32), dma(2)],
        (4 * rows * width * route_count, message_bytes, 0),
        near=(2,),
    )
    att_far = lax.ppermute(attended, AXES, off_chip)

    encoded, own, keyval, mixes = call(
        functools.partial(own_kernel, query_scale),
        [shape((rows, model)), shape((rows, width + model)), shape((rows, 2 * width)),
         shape((pairs, rows, 2 * LANES), jnp.float32)],
        [VMEM] * 4,
        (mesh_feats, attended, w_out_enc, w_qkv),
        [held(mesh_feats), held(w_out_enc), held(w_qkv), dma(3)],
        (8 * rows * model * width, 2 * model * (2 * rows + 4 * width), 0),
        near=(1,),
    )

    chip_kv = lax.ppermute(keyval, AXES, on_chip)
    place_index = lax.axis_index(AXES)
    odd = place_index % 2
    edges = jnp.stack([odd, (place_index + 2 * odd - 1) % (node_count + 1) < node_count]).astype(jnp.int32)
    processed = call(
        window_kernel,
        shape((rows, model)),
        VMEM,
        (edges, own, mixes, mesh_far, att_far, chip_kv, w_out_enc, w_qkv, w_out_proc),
        [held(chip_kv), held(w_out_enc), pltpu.VMEM((model, 2 * width), jnp.bfloat16), held(w_out_proc),
         pltpu.VMEM((rows, width), jnp.bfloat16), dma(4)],
        (16 * rows * model * width, 2 * model * (4 * rows + 5 * width), 3 * rows * rows * HEADS),
        near=range(1, 5),
    )
    return (encoded, processed)


def solution(mesh):
    rows = P(("groups", "outer", "inner"), None)
    return jax.shard_map(
        local,
        mesh=mesh,
        in_specs=(rows,) * 5 + (P(),) * 5,
        out_specs=(rows, rows),
        check_vma=False,
    )
```

```python
import functools
import math

import jax
import jax.numpy as jnp
from jax import lax
from jax.experimental import pallas as pl
from jax.experimental.pallas import tpu as pltpu
from jax.sharding import PartitionSpec as P


HEADS = 8
LANES = 128
NEG = -1e30
AXES = ("outer", "inner")
VMEM = pl.BlockSpec(memory_space=pltpu.VMEM)
SMEM = pl.BlockSpec(memory_space=pltpu.SMEM)
ANY = pl.BlockSpec(memory_space=pl.ANY)
HBM = pl.BlockSpec(memory_space=pltpu.HBM)
LIMIT = 50 << 20


def norm_rows(inputs):
    as_float = inputs.astype(jnp.float32)
    row_mean = jnp.mean(as_float, axis=-1, keepdims=True)
    centered = as_float - row_mean
    variance = jnp.mean(centered * centered, axis=-1, keepdims=True)
    return (centered * lax.rsqrt(variance + 1e-05)).astype(jnp.bfloat16)


def mm(a, b):
    return jnp.dot(a, b, preferred_element_type=jnp.float32)


def mm_nt(a, b):
    return lax.dot_general(a, b, (((1,), (1,)), ((), ())), preferred_element_type=jnp.float32)


def mm_tn(a, b):
    return lax.dot_general(a, b, (((0,), (0,)), ((), ())), preferred_element_type=jnp.float32)


def lane_group(shape, width):
    return lax.broadcasted_iota(jnp.int32, shape, len(shape) - 1) // width


def half_masks():
    low = (lane_group((1, LANES), LANES // 2) == 0).astype(jnp.float32)
    return low.astype(jnp.bfloat16), (1.0 - low).astype(jnp.bfloat16)


def fetch(pairs, sems):
    copies = [pltpu.make_async_copy(src, dst, sems.at[i]) for i, (src, dst) in enumerate(pairs)]
    for item in copies:
        item.start()
    return copies


def send_kernel(block_len, capacity, query_scale, routes_h, first_h, count_h, mesh_h, w_query_h, send, ranks,
                routes, first, count, mesh, w_query, tally, notes, sems):
    copies = fetch(
        [(mesh_h, mesh), (w_query_h, w_query), (routes_h, routes), (first_h, first), (count_h, count)], sems
    )
    route_count, block_count = routes.shape
    node_count = send.shape[0]
    pair_rows = capacity * block_len
    pairs = w_query.shape[1] // LANES
    note_rows = send.shape[1] - pairs * pair_rows

    def clear(i, carry):
        tally[i] = 0
        return carry

    lax.fori_loop(0, node_count, clear, 0)
    if node_count * capacity != block_count * route_count:
        send[...] = jnp.zeros(send.shape, send.dtype)
    notes[...] = jnp.zeros(notes.shape, notes.dtype)
    copies[0].wait()
    normed = norm_rows(mesh[...])
    for item in copies[1:]:
        item.wait()
    first_all = first[...]
    upper = first_all >= 256
    low_part = jnp.where(upper, first_all - 256, first_all).astype(jnp.float32)
    signed = jnp.where(upper, -count[...], count[...]).astype(jnp.float32)
    group = lane_group((1, LANES), block_len)
    per_tile = LANES // block_len
    queries = (mm(normed, w_query[...]) * query_scale).astype(jnp.bfloat16)
    for block in range(block_count):
        tile, spot = divmod(block, per_tile)
        cols = slice(tile * LANES, (tile + 1) * LANES)
        rows = slice(block * block_len, (block + 1) * block_len)
        for route in range(route_count):
            owner = routes[route, block]
            rank = tally[owner]
            tally[owner] = rank + 1
            ranks[route, block] = rank
            for pair in range(pairs):
                start = pl.multiple_of(pair * pair_rows + rank * block_len, block_len)
                send[owner, pl.ds(start, block_len), :] = queries[rows, pair * LANES:(pair + 1) * LANES]
            note = owner * note_rows + 2 * rank
            keep = group == spot
            notes[pl.ds(note, 1), :] = jnp.where(keep, low_part[route:route + 1, cols], 0.0)
            notes[pl.ds(note + 1, 1), :] = jnp.where(keep, signed[route:route + 1, cols], 0.0)
    for owner in range(node_count):
        send[owner, pairs * pair_rows:, :] = notes[owner * note_rows:(owner + 1) * note_rows, :].astype(jnp.bfloat16)


def grid_kernel(grid_h, w_kv_h, table, grid, w_kv, sems):
    copies = fetch([(grid_h, grid), (w_kv_h, w_kv)], sems)
    width = w_kv.shape[1] // 2
    copies[0].wait()
    normed = norm_rows(grid[...])
    copies[1].wait()
    grid_kv = mm(normed, w_kv[...]).astype(jnp.bfloat16)
    count = grid_kv.shape[0]
    masks = half_masks()
    for pair in range(width // LANES):
        key_pair = grid_kv[:, pair * LANES:(pair + 1) * LANES]
        value_pair = grid_kv[:, width + pair * LANES:width + (pair + 1) * LANES]
        for half in range(2):
            mask = masks[half]
            rows = slice(half * count, (half + 1) * count)
            table[pair, rows, :LANES] = value_pair * mask
            table[pair, rows, LANES:] = jnp.broadcast_to(mask, (count, LANES))
            table[pair, 2 * count:, half * LANES:(half + 1) * LANES] = key_pair * mask


def owner_kernel(block_len, capacity, chunk, recv, table_h, back_h, table, back, bias, sems, outs):
    node_count, message_rows, _ = recv.shape
    pairs, table_rows, _ = table.shape
    key_count = table_rows // 3
    pair_rows = capacity * block_len
    note_rows = message_rows - pairs * pair_rows
    group = chunk // pair_rows
    chunks = node_count // group
    copies = fetch([(table_h.at[pair], table.at[pair]) for pair in range(pairs)], sems)
    tags = recv[:, pairs * pair_rows:, :].reshape(node_count * note_rows, LANES)
    fold = (
        lax.broadcasted_iota(jnp.int32, (block_len, LANES), 1) % block_len
        == lax.broadcasted_iota(jnp.int32, (block_len, LANES), 0)
    ).astype(jnp.float32).astype(jnp.bfloat16)
    columns = mm_nt(fold, tags)
    key_pos = lax.broadcasted_iota(jnp.int32, (block_len, key_count), 1).astype(jnp.float32)

    def make_bias(index):
        for slot in range(index * group * capacity, (index + 1) * group * capacity):
            spot = slot // capacity * note_rows + 2 * (slot % capacity)
            low_part, signed = columns[:, spot:spot + 1], columns[:, spot + 1:spot + 2]
            begin = low_part + jnp.where(signed < 0, 256.0, 0.0)
            end = begin + jnp.maximum(jnp.abs(signed), 1.0)
            inside = (key_pos >= begin) & (key_pos < end)
            bias[slot * block_len:(slot + 1) * block_len, :] = jnp.where(inside, 0.0, NEG)

    for index in range(chunks):
        make_bias(index)
    low_half = lane_group((chunk, LANES), LANES // 2) == 0
    half_lane = lane_group((HEADS, LANES), LANES // 2)
    log_width = LANES // 2 // pairs
    log_group = lane_group((chunk, LANES), log_width) % pairs
    pick_row = lax.broadcasted_iota(jnp.int32, (HEADS, LANES), 0)
    pick_lane = lax.broadcasted_iota(jnp.int32, (HEADS, LANES), 1)
    pick = (pick_lane == pick_row % 2 * (LANES // 2) + pick_row // 2 * log_width).astype(jnp.float32).astype(jnp.bfloat16)
    steps = [(index, head) for index in range(chunks) for head in range(HEADS)]
    scores, softs, mixes, held_logs = {}, {}, {}, {}
    moves = []
    for turn in range(len(steps) + 4):
        if turn < len(steps):
            index, head = steps[turn]
            pair, half = divmod(head, 2)
            if index == 0 and half == 0:
                copies[pair].wait()
            span = slice(index * group, (index + 1) * group)
            rows = recv[span, pair * pair_rows:(pair + 1) * pair_rows, :].reshape(chunk, LANES)
            keys = table[pair, 2 * key_count:, half * LANES:(half + 1) * LANES]
            scores[turn] = mm_nt(rows, keys) + bias[index * chunk:(index + 1) * chunk, :]
        item = scores.pop(turn - 2, None)
        if item is not None:
            top = jnp.max(item, axis=-1, keepdims=True)
            softs[turn - 2] = (top, jnp.exp2(item - top).astype(jnp.bfloat16))
        step = turn - 4
        if step < 0:
            continue
        index, head = steps[step]
        pair, half = divmod(head, 2)
        mixes[step] = mm(softs[step][1], table[pair, half * key_count:(half + 1) * key_count, :])
        if half == 0:
            continue
        mixed = mixes.pop(step - 1) + mixes.pop(step)
        total = mixed[:, LANES:]
        span = slice(index * group, (index + 1) * group)
        part = slice(pair * pair_rows, (pair + 1) * pair_rows)
        back[span, part, :] = (mixed[:, :LANES] / total).astype(jnp.bfloat16).reshape(group, pair_rows, LANES)
        logs = jnp.where(low_half, softs.pop(step - 1)[0], softs.pop(step)[0]) + jnp.log2(total)
        held_logs[index] = jnp.where(log_group == pair, logs, held_logs[index]) if pair else logs
        last = index == chunks - 1
        if last and pair < pairs - 1:
            place = (pl.ds(index * group, group), pl.ds(pair * pair_rows, pair_rows))
            moves.append(pltpu.make_async_copy(back.at[place], back_h.at[place], outs.at[chunks + pair]))
            moves[-1].start()
        if pair < pairs - 1:
            continue
        logs = held_logs.pop(index)
        high = logs.astype(jnp.bfloat16)
        log_high = mm_nt(pick, high)
        log_low = mm_nt(pick, (logs - high.astype(jnp.float32)).astype(jnp.bfloat16))
        for offset in range(group):
            lane = offset * pair_rows
            tile, shift = lane // LANES, lane % LANES
            high = log_high[:, tile * LANES:(tile + 1) * LANES]
            low = log_low[:, tile * LANES:(tile + 1) * LANES]
            if shift:
                high = pltpu.roll(high, LANES - shift, 1)
            low_shift = (LANES // 2 - shift) % LANES
            if low_shift:
                low = pltpu.roll(low, low_shift, 1)
            back[index * group + offset, pairs * pair_rows:pairs * pair_rows + HEADS, :] = jnp.where(
                half_lane == 0, high, low
            ).astype(jnp.bfloat16)
        first_row = (pairs - 1) * pair_rows if last else 0
        place = (pl.ds(index * group, group), pl.ds(first_row, message_rows - first_row))
        moves.append(pltpu.make_async_copy(back.at[place], back_h.at[place], outs.at[index]))
        moves[-1].start()
    for item in moves:
        item.wait()


def combine_kernel(block_len, capacity, routes_h, ranks_h, back, attended, routes, ranks, logs, sems):
    node_count, _, _ = back.shape
    width = attended.shape[1]
    pairs = width // LANES
    pair_rows = capacity * block_len
    copies = fetch([(routes_h, routes), (ranks_h, ranks)], sems)
    route_count, block_count = routes.shape
    halves = back[:, pairs * pair_rows:pairs * pair_rows + HEADS, :].astype(jnp.float32).reshape(node_count * HEADS, LANES)
    logs[...] = halves + pltpu.roll(halves, LANES // 2, 1)
    for item in copies:
        item.wait()
    group = lane_group((HEADS, LANES), block_len)
    per_tile = LANES // block_len
    tiles = block_count // per_tile
    route_logs = []
    for route in range(route_count):
        parts = []
        for tile in range(tiles):
            gathered = jnp.zeros((HEADS, LANES), jnp.float32)
            for spot in range(per_tile):
                block = tile * per_tile + spot
                start = pl.multiple_of(routes[route, block] * HEADS, HEADS)
                shift = (spot + per_tile - ranks[route, block]) * block_len % LANES
                moved = pltpu.roll(logs[pl.ds(start, HEADS), :], shift, 1)
                gathered = jnp.where(group == spot, moved, gathered)
            parts.append(gathered)
        route_logs.append(jnp.concatenate(parts, axis=1))
    best = functools.reduce(jnp.maximum, route_logs)
    terms = [jnp.exp2(item - best) for item in route_logs]
    total = functools.reduce(jnp.add, terms)
    spread = (
        lax.broadcasted_iota(jnp.int32, (2 * HEADS, width), 1) // (width // HEADS)
        == lax.broadcasted_iota(jnp.int32, (2 * HEADS, width), 0) % HEADS
    ).astype(jnp.float32).astype(jnp.bfloat16)
    weights = []
    for item in terms:
        share = item / total
        high = share.astype(jnp.bfloat16).astype(jnp.float32)
        both = jnp.concatenate([high, share - high], axis=0).astype(jnp.bfloat16)
        weights.append(mm_tn(both, spread))
    for block in range(block_count):
        rows = slice(block * block_len, (block + 1) * block_len)
        for pair in range(pairs):
            lanes = slice(pair * LANES, (pair + 1) * LANES)
            acc = None
            for route in range(route_count):
                start = pl.multiple_of(pair * pair_rows + ranks[route, block] * block_len, block_len)
                piece = back[routes[route, block], pl.ds(start, block_len), :].astype(jnp.float32)
                piece = piece * weights[route][rows, lanes]
                acc = piece if acc is None else acc + piece
            attended[rows, lanes] = acc.astype(jnp.bfloat16)


def own_kernel(query_scale, mesh_h, attended, w_out_h, w_qkv_h, encoded, own, keyval, mixes,
               mesh, w_out, w_qkv, sems):
    width = attended.shape[1]
    query_part, other_part = pl.ds(0, width), pl.ds(width, 2 * width)
    copies = fetch(
        [
            (w_out_h, w_out),
            (mesh_h, mesh),
            (w_qkv_h.at[:, query_part], w_qkv.at[:, query_part]),
            (w_qkv_h.at[:, other_part], w_qkv.at[:, other_part]),
        ],
        sems,
    )
    for item in copies[:2]:
        item.wait()
    rows = (mesh[...].astype(jnp.float32) + mm(attended[...], w_out[...])).astype(jnp.bfloat16)
    encoded[...] = rows
    own[:, width:] = rows
    normed = norm_rows(rows)
    copies[2].wait()
    query = (mm(normed, w_qkv[:, :width]) * query_scale).astype(jnp.bfloat16)
    own[:, :width] = query
    copies[3].wait()
    keyval[...] = mm(normed, w_qkv[:, width:]).astype(jnp.bfloat16)
    low_half = lane_group((rows.shape[0], LANES), LANES // 2) == 0
    masks = half_masks()
    scores, softs, mixed = {}, {}, {}
    for turn in range(HEADS + 2):
        if turn < HEADS:
            lanes = slice(turn // 2 * LANES, (turn // 2 + 1) * LANES)
            scores[turn] = mm_nt(query[:, lanes], keyval[:, lanes] * masks[turn % 2])
        head = turn - 1
        if 0 <= head < HEADS:
            item = scores.pop(head)
            top = jnp.max(item, axis=-1, keepdims=True)
            softs[head] = (top, jnp.exp2(item - top).astype(jnp.bfloat16))
        head = turn - 2
        if head < 0:
            continue
        pair, half = divmod(head, 2)
        value = keyval[:, width + pair * LANES:width + (pair + 1) * LANES]
        table = jnp.concatenate([value * masks[half], jnp.broadcast_to(masks[half], value.shape)], axis=1)
        mixed[half] = mm(softs[head][1], table)
        if half:
            total = mixed[0] + mixed[1]
            mixes[pair, :, :LANES] = total[:, :LANES] / total[:, LANES:]
            top = jnp.where(low_half, softs.pop(head - 1)[0], softs.pop(head)[0])
            mixes[pair, :, LANES:] = top + jnp.log2(total[:, LANES:])


def window_kernel(edges, own, mixes, mesh_far, att_far, chip_kv_h, w_out_h, w_qkv_h, w_proc_h, processed,
                  chip_kv, w_out, w_near, w_proc, mixed, chip_all, sems):
    rows, width = mixed.shape
    copies = fetch(
        [
            (chip_kv_h, chip_kv),
            (w_out_h, w_out),
            (w_qkv_h.at[:, pl.ds(width, 2 * width)], w_near),
            (w_proc_h, w_proc),
        ],
        sems,
    )
    masks = half_masks()
    copies[0].wait()
    for head in range(HEADS):
        lanes = slice(head // 2 * LANES, (head // 2 + 1) * LANES)
        chip_all[head] = mm_nt(own[:, lanes], chip_kv[:, lanes] * masks[head % 2])
    copies[1].wait()
    far = (mesh_far[...].astype(jnp.float32) + mm(att_far[...], w_out[...])).astype(jnp.bfloat16)
    normed = norm_rows(far)
    copies[2].wait()
    far_kv = mm(normed, w_near[...]).astype(jnp.bfloat16)
    behind = lax.broadcasted_iota(jnp.int32, (rows, rows), 1) >= lax.broadcasted_iota(jnp.int32, (rows, rows), 0)
    in_far = behind.astype(jnp.int32) != edges[0]
    bias = jnp.where(in_far & (edges[1] == 0), NEG, 0.0)
    low_half = lane_group((rows, LANES), LANES // 2) == 0
    masks = half_masks()
    scores, softs, sums = {}, {}, {}
    for turn in range(HEADS + 2):
        if turn < HEADS:
            lanes = slice(turn // 2 * LANES, (turn // 2 + 1) * LANES)
            far_scores = mm_nt(own[:, lanes], far_kv[:, lanes] * masks[turn % 2])
            scores[turn] = jnp.where(in_far, far_scores, chip_all[turn]) + bias
        head = turn - 1
        if 0 <= head < HEADS:
            item = scores.pop(head)
            top = jnp.max(item, axis=-1, keepdims=True)
            term = jnp.exp2(item - top)
            first = jnp.where(in_far, term, 0.0)
            softs[head] = (top, jnp.concatenate([first, term - first], axis=1).astype(jnp.bfloat16))
        head = turn - 2
        if head < 0:
            continue
        pair, half = divmod(head, 2)
        lanes = slice(width + pair * LANES, width + (pair + 1) * LANES)
        value = jnp.concatenate([far_kv[:, lanes], chip_kv[:, lanes]], axis=0)
        table = jnp.concatenate([value * masks[half], jnp.broadcast_to(masks[half], value.shape)], axis=1)
        sums[half] = mm(softs[head][1], table)
        if half:
            top = jnp.where(low_half, softs.pop(head - 1)[0], softs.pop(head)[0])
            own_log = mixes[pair, :, LANES:]
            best = jnp.maximum(top, own_log)
            near_part, own_part = jnp.exp2(top - best), jnp.exp2(own_log - best)
            total = sums[0] + sums[1]
            share = total[:, :LANES] * near_part + mixes[pair, :, :LANES] * own_part
            count = total[:, LANES:] * near_part + own_part
            mixed[:, pair * LANES:(pair + 1) * LANES] = (share / count).astype(jnp.bfloat16)
    copies[3].wait()
    processed[...] = (own[:, width:].astype(jnp.float32) + mm(mixed[...], w_proc[...])).astype(jnp.bfloat16)


def call(kernel, outs, out_specs, operands, scratch, cost, limit=LIMIT, near=()):
    return pl.pallas_call(
        kernel,
        out_shape=outs,
        in_specs=[SMEM if item.shape == (2,) else VMEM if i in near else ANY for i, item in enumerate(operands)],
        out_specs=out_specs,
        scratch_shapes=scratch,
        cost_estimate=pl.CostEstimate(flops=cost[0], bytes_accessed=cost[1], transcendentals=cost[2]),
        compiler_params=pltpu.CompilerParams(vmem_limit_bytes=limit),
    )(*operands)


def shape(dims, dtype=jnp.bfloat16):
    return jax.ShapeDtypeStruct(dims, dtype)


def held(item):
    return pltpu.VMEM(item.shape, item.dtype)


def dma(count):
    return pltpu.SemaphoreType.DMA((count,))


def local(grid_feats, mesh_feats, routes, edge_first, edge_count, w_query, w_kv, w_out_enc, w_qkv, w_out_proc):
    width = w_query.shape[1]
    model = mesh_feats.shape[1]
    query_scale = math.log2(math.e) / math.sqrt(width // HEADS)
    node_count = lax.axis_size("outer") * lax.axis_size("inner")
    block_count, route_count = routes.shape
    rows = mesh_feats.shape[0]
    key_count = grid_feats.shape[0]
    block_len = rows // block_count
    capacity = max(1, (block_count * route_count + node_count - 1) // node_count)
    pairs = width // LANES
    pair_rows = capacity * block_len
    note_rows = max(8, -(-2 * capacity // 8) * 8)
    message = shape((node_count, pairs * pair_rows + note_rows, LANES))
    message_bytes = 2 * math.prod(message.shape)
    routes_t, first_t, count_t = routes.T, edge_first.T, edge_count.T
    ranks_shape = shape(routes_t.shape, jnp.int32)
    in_smem = pltpu.SMEM(routes_t.shape, jnp.int32)
    place = (block_len, capacity)

    send, ranks = call(
        functools.partial(send_kernel, *place, query_scale),
        [message, ranks_shape],
        [VMEM, SMEM],
        (routes_t, first_t, count_t, mesh_feats, w_query),
        [in_smem, held(first_t), held(count_t), held(mesh_feats), held(w_query), pltpu.SMEM((node_count,), jnp.int32),
         pltpu.VMEM((node_count * note_rows, LANES), jnp.float32), dma(5)],
        (2 * rows * model * width, 2 * model * (rows + width) + message_bytes, 0),
        None,
    )
    recv = lax.all_to_all(send, AXES, split_axis=0, concat_axis=0, tiled=True)

    table = call(
        grid_kernel,
        shape((pairs, 3 * key_count, 2 * LANES)),
        VMEM,
        (grid_feats, w_kv),
        [held(grid_feats), held(w_kv), dma(2)],
        (4 * key_count * model * width, 2 * model * (key_count + 2 * width) + 12 * key_count * width, 0),
        None,
    )

    on_chip = [(i, i ^ 1) for i in range(node_count)]
    off_chip = [(i, i + 1) for i in range(1, node_count - 1, 2)] + [(i + 1, i) for i in range(1, node_count - 1, 2)]
    late_mesh, table = lax.optimization_barrier((mesh_feats, table))
    mesh_far = lax.ppermute(late_mesh, AXES, off_chip)

    chunk = math.gcd(node_count * pair_rows, 512)
    back = call(
        functools.partial(owner_kernel, *place, chunk),
        message,
        HBM,
        (recv, table),
        [held(table), held(message), pltpu.VMEM((node_count * pair_rows, key_count), jnp.float32), dma(pairs),
         dma(node_count * pair_rows // chunk + pairs)],
        (4 * node_count * pair_rows * key_count * width, 2 * message_bytes, node_count * pair_rows * key_count * HEADS),
        near=(0,),
    )
    back = lax.all_to_all(back, AXES, split_axis=0, concat_axis=0, tiled=True)

    attended = call(
        functools.partial(combine_kernel, *place),
        shape((rows, width)),
        VMEM,
        (routes_t, ranks, back),
        [in_smem, in_smem, pltpu.VMEM((node_count * HEADS, LANES), jnp.float32), dma(2)],
        (4 * rows * width * route_count, message_bytes, 0),
        near=(2,),
    )
    att_far = lax.ppermute(attended, AXES, off_chip)

    encoded, own, keyval, mixes = call(
        functools.partial(own_kernel, query_scale),
        [shape((rows, model)), shape((rows, width + model)), shape((rows, 2 * width)),
         shape((pairs, rows, 2 * LANES), jnp.float32)],
        [VMEM] * 4,
        (mesh_feats, attended, w_out_enc, w_qkv),
        [held(mesh_feats), held(w_out_enc), held(w_qkv), dma(4)],
        (8 * rows * model * width, 2 * model * (2 * rows + 4 * width), 0),
        near=(1,),
    )

    chip_kv = lax.ppermute(keyval, AXES, on_chip)
    place_index = lax.axis_index(AXES)
    odd = place_index % 2
    edges = jnp.stack([odd, (place_index + 2 * odd - 1) % (node_count + 1) < node_count]).astype(jnp.int32)
    processed = call(
        window_kernel,
        shape((rows, model)),
        VMEM,
        (edges, own, mixes, mesh_far, att_far, chip_kv, w_out_enc, w_qkv, w_out_proc),
        [held(chip_kv), held(w_out_enc), pltpu.VMEM((model, 2 * width), jnp.bfloat16), held(w_out_proc),
         pltpu.VMEM((rows, width), jnp.bfloat16), pltpu.VMEM((HEADS, rows, rows), jnp.float32), dma(4)],
        (16 * rows * model * width, 2 * model * (4 * rows + 5 * width), 3 * rows * rows * HEADS),
        near=range(1, 5),
    )
    return (encoded, processed)


def solution(mesh):
    rows = P(("groups", "outer", "inner"), None)
    return jax.shard_map(
        local,
        mesh=mesh,
        in_specs=(rows,) * 5 + (P(),) * 5,
        out_specs=(rows, rows),
        check_vma=False,
    )
```
